512 devices in a mesh: head: 16 (over y_lo, z), key: 32 (over x, y_hi, core).
Axes of the slice: x: 4, y: 8 (y_hi: 4, y_lo: 2; y = y_hi * 2 + y_lo), z: 8, core: 2. Of those that a mesh axis runs over, the one named last changes fastest.
Arguments:
- query_pos: int32 [256], replicated, may hold values from 16384 to 65535
- mla_query: bfloat16 [128, 256, 576], P('head'), may hold values from -94 to 94
- latent_keys: bfloat16 [65536, 576], P('key'), may hold values from -7 to 7
- index_query: bfloat16 [256, 64, 128], P('head'), may hold values from -48 to 48
- index_keys: bfloat16 [65536, 128], P('key'), may hold values from -7 to 7
- index_weights: float32 [256, 64], P('head'), may hold values from -1.8 to 1.8
Outputs:
- query_grads: float32 [256, 64, 128], P('head')
- key_grads: float32 [65536, 128], P(('key', 'head'))
The draws below stay inside these ranges and needn't reach their ends.
All inputs are finite; a program needn't handle non-finite values.
Results may differ from the reference program's by a relative error of at most 0.014.
Values sent between devices are 32-bit elements; how exact they have to be, the bound alone decides.
No kernel may reach another device: no remote copies, remote signals or barrier semaphores. Data moves between devices by JAX's collectives and lax.ppermute only.
A program may use at most 128 MiB of HBM per device.

```python
import jax
import jax.numpy as jnp
from jax import lax

HEADS = 128
LATENT = 576
IHEADS = 64
IDIM = 128
ROWS = 256
KEYS = 65536


def chosen_keys(key):
    offsets = jax.random.randint(jax.random.fold_in(key, 7), (4,), 0, KEYS // 64)
    first_key = jnp.arange(4, dtype=jnp.int32) * (KEYS // 32) + offsets
    return (first_key, first_key + KEYS // 64)


def chosen_rows():
    return jnp.arange(4, dtype=jnp.int32) * (ROWS // 4)


def target_levels():
    return jnp.linspace(30.0, 90.0, 4)


def near_copy(base, gap_key, noise_key, levels, width):
    gaps = jax.random.uniform(gap_key, (4,), jnp.float32, 1.5, 2.5)
    noise = jnp.clip(jax.random.normal(noise_key, (4, width), jnp.float32), -3.0, 3.0)
    noise = noise * (0.3 * width ** 0.5) / levels[:, None]
    return base * (1.0 - gaps / levels)[:, None] + noise


def mla_pair(key):
    streams = jax.random.split(jax.random.fold_in(key, 101), 5)
    latent = jnp.clip(jax.random.normal(streams[0], (KEYS, LATENT), jnp.float32), -6.0, 6.0)
    queries = jnp.clip(jax.random.normal(streams[1], (HEADS, ROWS, LATENT), jnp.float32), -6.0, 6.0)
    first_key, second = chosen_keys(key)
    levels = target_levels()
    latent = latent.at[second].set(near_copy(latent[first_key], streams[2], streams[3], levels, LATENT))
    head_factor = jax.random.uniform(streams[4], (HEADS, 4), jnp.float32, 0.85, 1.15)
    strength = levels * 192.0 ** 0.5 / LATENT
    planted = strength[None, :, None] * head_factor[:, :, None] * latent[first_key][None]
    queries = queries.at[:, chosen_rows()].set(planted)
    return (latent, queries)


def index_triple(key):
    streams = jax.random.split(jax.random.fold_in(key, 202), 5)
    keys_drawn = jnp.clip(jax.random.normal(streams[0], (KEYS, IDIM), jnp.float32), -6.0, 6.0)
    queries = jnp.clip(jax.random.normal(streams[1], (ROWS, IHEADS, IDIM), jnp.float32), -6.0, 6.0)
    weights = 0.3 * jnp.clip(jax.random.normal(streams[2], (ROWS, IHEADS), jnp.float32), -6.0, 6.0)
    first_key, second = chosen_keys(key)
    levels = target_levels()
    keys_drawn = keys_drawn.at[second].set(near_copy(keys_drawn[first_key], streams[3], streams[4], levels, IDIM))
    strength = levels * 128.0 ** 0.5 / (0.125 * IHEADS * IDIM)
    planted = strength[:, None, None] * jnp.broadcast_to(keys_drawn[first_key][:, None, :], (4, IHEADS, IDIM))
    queries = queries.at[chosen_rows()].set(planted)
    weights = weights.at[chosen_rows()].set(jnp.full((4, IHEADS), 0.125, jnp.float32))
    return (keys_drawn, queries, weights)


def draw_mla_query(key, part):
    return mla_pair(key)[1].astype(jnp.bfloat16)


def draw_latent_keys(key, part):
    return mla_pair(key)[0].astype(jnp.bfloat16)


def draw_index_query(key, part):
    return index_triple(key)[1].astype(jnp.bfloat16)


def draw_index_keys(key, part):
    return index_triple(key)[0].astype(jnp.bfloat16)


def draw_index_weights(key, part):
    return index_triple(key)[2]


def place_ends(values, own_key, smallest, largest):
    longest = values.shape.index(max(values.shape))
    spots = []
    for shift in (0, 1):
        where = [jax.random.randint(jax.random.fold_in(own_key, axis), (), 0, length) for axis, length in enumerate(values.shape)]
        where[longest] = (where[longest] + shift) % values.shape[longest]
        spots.append(tuple(where))
    return values.at[spots[0]].set(smallest).at[spots[1]].set(largest)


def setup_inputs(seed: int = 0) -> dict:
    arg_keys = jax.random.split(jax.random.key(seed), 7)
    query_pos = place_ends(jax.random.randint(arg_keys[0], (ROWS,), KEYS // 4, KEYS), jax.random.fold_in(arg_keys[0], 1), KEYS // 4, KEYS - 1).astype(jnp.int32)
    mla_query = draw_mla_query(jax.random.fold_in(arg_keys[6], 71), 0)
    latent_keys = draw_latent_keys(jax.random.fold_in(arg_keys[6], 71), 0)
    index_query = draw_index_query(jax.random.fold_in(arg_keys[6], 71), 0)
    index_keys = draw_index_keys(jax.random.fold_in(arg_keys[6], 71), 0)
    index_weights = draw_index_weights(jax.random.fold_in(arg_keys[6], 71), 0)
    return dict(query_pos=query_pos, mla_query=mla_query, latent_keys=latent_keys, index_query=index_query, index_keys=index_keys, index_weights=index_weights)


attn_scale = 192.0 ** -0.5
index_scale = 128.0 ** -0.5
masked_fill = -1.0e30


def reference(query_pos, mla_query, latent_keys, index_query, index_keys, index_weights):
    visible = jnp.arange(KEYS, dtype=jnp.int32)[None, :] <= query_pos[:, None]

    def add_head(summed, q_head):
        scores = jnp.dot(q_head, latent_keys.T, preferred_element_type=jnp.float32) * attn_scale
        masked = jnp.where(visible, scores, masked_fill)
        highest = jnp.max(masked, axis=-1, keepdims=True)
        weights = jnp.where(visible, jnp.exp(masked - highest), 0.0)
        weights = weights / jnp.sum(weights, axis=-1, keepdims=True)
        return summed + weights / HEADS, None

    target, _ = lax.scan(add_head, jnp.zeros((ROWS, KEYS), jnp.float32), mla_query)
    keys_wide = index_keys.astype(jnp.float32)

    def row_block(carry, pieces):
        queries, weights_idx, target_rows, seen = pieces
        index_dots = jnp.einsum('rjd,kd->rjk', queries.astype(jnp.float32), keys_wide)
        logits = index_scale * jnp.einsum('rj,rjk->rk', weights_idx, jnp.maximum(index_dots, 0.0), precision=lax.Precision.HIGHEST)
        masked = jnp.where(seen, logits, masked_fill)
        highest = jnp.max(masked, axis=-1, keepdims=True)
        index_probs = jnp.where(seen, jnp.exp(masked - highest), 0.0)
        index_probs = index_probs / jnp.sum(index_probs, axis=-1, keepdims=True)
        slope = (index_probs - target_rows) * KEYS
        coef = jnp.where(index_dots > 0, slope[:, None, :] * weights_idx[:, :, None] * index_scale, 0.0).astype(jnp.bfloat16)
        coef_wide = coef.astype(jnp.float32)
        grad_rows = jnp.einsum('rjk,kd->rjd', coef_wide, keys_wide)
        grad_keys = jnp.einsum('rjk,rjd->kd', coef_wide, queries.astype(jnp.float32))
        return carry + grad_keys, grad_rows

    def grouped(array):
        return array.reshape((ROWS // 8, 8) + array.shape[1:])

    key_grads, query_grads = lax.scan(row_block, jnp.zeros((KEYS, IDIM), jnp.float32),
                                      (grouped(index_query), grouped(index_weights), grouped(target), grouped(visible)))
    return query_grads.reshape(ROWS, IHEADS, IDIM), key_grads
```

```python
import math

import jax
import jax.numpy as jnp
from jax import lax
from jax.experimental import pallas as pl
from jax.experimental.pallas import tpu as pltpu
from jax.sharding import Mesh
from jax.sharding import PartitionSpec as P

HEADS = 128
KEY = ("x", "yh", "core")
FAR = ("x", "yh")
HEAD = ("yl", "z")
LOG2E = math.log2(math.e)
attn_scale = 192.0 ** (-0.5) * LOG2E
index_scale = 128.0 ** (-0.5)
masked_fill = -1e30
NT = (((1,), (1,)), ((), ()))
NN = (((1,), (0,)), ((), ()))
TN = (((0,), (0,)), ((), ()))


def dot(a, b, dims):
    return lax.dot_general(a, b, dims, preferred_element_type=jnp.float32)


def params(semantics=("arbitrary",)):
    return pltpu.CompilerParams(
        dimension_semantics=semantics, vmem_limit_bytes=48 * 1024 * 1024
    )


def score_stats_kernel(pos_ref, q_ref, k_ref, out_ref, *, tile):
    head = pl.program_id(0)
    keys = k_ref.shape[0]
    pos = pos_ref[...]
    q = q_ref[0]
    highs, sums = [], []
    for start in range(0, keys, tile):
        scores = dot(k_ref[start : start + tile, :], q, NT) * attn_scale
        ids = lax.broadcasted_iota(jnp.int32, scores.shape, 0)
        scores = jnp.where(ids <= pos - start, scores, masked_fill)
        high = jnp.max(scores, axis=0, keepdims=True)
        highs.append(high)
        sums.append(jnp.sum(jnp.exp2(scores - high), axis=0, keepdims=True))
    high = highs[0]
    for other in highs[1:]:
        high = jnp.maximum(high, other)
    total = sum(s * jnp.exp2(h - high) for h, s in zip(highs, sums))
    line = high + jnp.log2(total)
    out_ref[:, pl.ds(head, 1), :] = jnp.broadcast_to(line[None], (out_ref.shape[0], 1, line.shape[1]))


def score_stats(rel_pos, q, k, copies):
    heads, rows, width = q.shape
    keys = k.shape[0]
    return pl.pallas_call(
        lambda *refs: score_stats_kernel(*refs, tile=512),
        grid=(heads,),
        in_specs=[
            pl.BlockSpec((1, rows), lambda h: (0, 0)),
            pl.BlockSpec((1, rows, width), lambda h: (h, 0, 0)),
            pl.BlockSpec((keys, width), lambda h: (0, 0)),
        ],
        out_specs=pl.BlockSpec((copies, heads, rows), lambda h: (0, 0, 0)),
        out_shape=jax.ShapeDtypeStruct((copies, heads, rows), jnp.float32),
        compiler_params=params(),
        cost_estimate=pl.CostEstimate(
            flops=2 * heads * rows * keys * width, transcendentals=heads * rows * keys, bytes_accessed=6 << 20
        ),
        name="score_stats",
    )(rel_pos.reshape(1, rows), q, k)


def head_share_kernel(stats_ref, pos_ref, q_ref, k_ref, out_ref, col_ref):
    heads = q_ref.shape[0]
    tile = k_ref.shape[0]
    step = pl.program_id(0)

    @pl.when(step == 0)
    def _():
        stats = stats_ref[...]
        high = jnp.max(stats, axis=0)
        total = jnp.sum(jnp.exp2(stats - high[None]), axis=0)
        line = high + jnp.log2(total) + math.log2(HEADS)
        col_ref[:, :heads] = jnp.transpose(line)

    k = k_ref[...]
    total = None
    for head in range(heads):
        scores = dot(q_ref[head], k, NT)
        part = jnp.exp2(scores * attn_scale - col_ref[:, head : head + 1])
        total = part if total is None else total + part
    ids = lax.broadcasted_iota(jnp.int32, total.shape, 1) + step * tile
    out_ref[...] = jnp.where(ids <= pos_ref[...], total, 0.0)


def head_share(stats, rel_pos, q, k):
    heads, rows, width = q.shape
    keys = k.shape[0]
    copies = stats.shape[0]
    tile = 256
    return pl.pallas_call(
        head_share_kernel,
        grid=(keys // tile,),
        in_specs=[
            pl.BlockSpec((copies, heads, rows), lambda t: (0, 0, 0)),
            pl.BlockSpec((rows, 1), lambda t: (0, 0)),
            pl.BlockSpec((heads, rows, width), lambda t: (0, 0, 0)),
            pl.BlockSpec((tile, width), lambda t: (t, 0)),
        ],
        out_specs=pl.BlockSpec((rows, tile), lambda t: (0, t)),
        out_shape=jax.ShapeDtypeStruct((rows, keys), jnp.float32),
        scratch_shapes=[pltpu.VMEM((rows, 128), jnp.float32)],
        compiler_params=params(),
        cost_estimate=pl.CostEstimate(
            flops=2 * heads * rows * keys * width, transcendentals=heads * rows * keys, bytes_accessed=8 << 20
        ),
        name="head_share",
    )(stats, rel_pos.reshape(rows, 1), q, k)


def index_logits_kernel(pos_ref, q_ref, w_ref, k_ref, logit_ref, stat_ref):
    rows = pos_ref.shape[0]
    iheads = q_ref.shape[0] // rows
    keys = k_ref.shape[0]
    tile = 512
    for start in range(0, keys, tile):
        k = k_ref[start : start + tile, :]
        lines = []
        for row in range(rows):
            own = slice(row * iheads, (row + 1) * iheads)
            dots = dot(q_ref[own, :], k, NT)
            lines.append(
                jnp.sum(jnp.maximum(dots, 0.0) * w_ref[own, :], axis=0, keepdims=True)
            )
        logits = jnp.concatenate(lines, axis=0) * (index_scale * LOG2E)
        ids = lax.broadcasted_iota(jnp.int32, logits.shape, 1) + start
        logit_ref[:, start : start + tile] = jnp.where(ids <= pos_ref[...], logits, masked_fill)
    logits = logit_ref[...]
    high = jnp.max(logits, axis=1, keepdims=True)
    total = jnp.sum(jnp.exp2(logits - high), axis=1, keepdims=True)
    stat_ref[...] = jnp.broadcast_to(high + jnp.log2(total), stat_ref.shape)


def index_logits(row_pos, q, w, k):
    rows, iheads, width = q.shape
    keys = k.shape[0]
    return pl.pallas_call(
        index_logits_kernel,
        out_shape=(
            jax.ShapeDtypeStruct((rows, keys), jnp.float32),
            jax.ShapeDtypeStruct((rows, 128), jnp.float32),
        ),
        compiler_params=pltpu.CompilerParams(vmem_limit_bytes=48 * 1024 * 1024),
        cost_estimate=pl.CostEstimate(
            flops=2 * rows * iheads * keys * width, transcendentals=rows * keys, bytes_accessed=1 << 20
        ),
        name="index_logits",
    )(row_pos.reshape(rows, 1), q.reshape(rows * iheads, width), w.reshape(rows * iheads, 1), k)


def gradients_kernel(parts_ref, logit_ref, stat_ref, q_ref, w_ref, k_ref, rows_ref, keys_ref, *, count):
    step = pl.program_id(0)
    rows = logit_ref.shape[0]
    iheads = q_ref.shape[0] // rows
    target = jnp.sum(parts_ref[...], axis=0)
    probs = jnp.exp2(logit_ref[...] - stat_ref[...])
    slope = (probs - target) * count
    k = k_ref[...]
    coefs = []
    for row in range(rows):
        own = slice(row * iheads, (row + 1) * iheads)
        dots = dot(q_ref[own, :], k, NT)
        coef = jnp.where(dots > 0, slope[row : row + 1, :] * w_ref[own, :] * index_scale, 0.0)
        coefs.append(coef.astype(jnp.bfloat16))
    coef = jnp.concatenate(coefs, axis=0)
    keys_ref[...] = dot(coef, q_ref[...], TN)
    part = dot(coef, k, NN)

    @pl.when(step == 0)
    def _():
        rows_ref[...] = part

    @pl.when(step > 0)
    def _():
        rows_ref[...] += part


def gradients(parts, logits, stat, q, w, k, count):
    rows, iheads, width = q.shape
    keys = k.shape[0]
    tile = 512
    flat = rows * iheads
    return pl.pallas_call(
        lambda *refs: gradients_kernel(*refs, count=float(count)),
        grid=(keys // tile,),
        in_specs=[
            pl.BlockSpec((parts.shape[0], rows, tile), lambda t: (0, 0, t)),
            pl.BlockSpec((rows, tile), lambda t: (0, t)),
            pl.BlockSpec((rows, 1), lambda t: (0, 0)),
            pl.BlockSpec((flat, width), lambda t: (0, 0)),
            pl.BlockSpec((flat, 1), lambda t: (0, 0)),
            pl.BlockSpec((tile, width), lambda t: (t, 0)),
        ],
        out_specs=(
            pl.BlockSpec((flat, width), lambda t: (0, 0)),
            pl.BlockSpec((tile, width), lambda t: (t, 0)),
        ),
        out_shape=(
            jax.ShapeDtypeStruct((flat, width), jnp.float32),
            jax.ShapeDtypeStruct((keys, width), jnp.float32),
        ),
        compiler_params=params(),
        cost_estimate=pl.CostEstimate(
            flops=6 * flat * keys * width, transcendentals=rows * keys, bytes_accessed=4 << 20
        ),
        name="gradients",
    )(parts, logits, stat, q.reshape(flat, width), w.reshape(flat, 1), k)


def exchanged(parts, axis):
    return lax.all_to_all(parts, axis, split_axis=0, concat_axis=0, tiled=True)


def spread(shard, axis):
    size = lax.axis_size(axis)
    return exchanged(jnp.broadcast_to(shard[None], (size, *shard.shape)), axis)


def summed(shard, axis):
    size = lax.axis_size(axis)
    return exchanged(shard.reshape(size, -1, shard.shape[-1]), axis).sum(axis=0)


def shards(query_pos, mla_query, latent_keys, index_query, index_keys, index_weights):
    keys = latent_keys.shape[0]
    rows = index_query.shape[0]
    heads_axis = lax.axis_size(HEAD)
    rel_pos = query_pos - lax.axis_index(KEY) * keys
    row_pos = lax.dynamic_slice_in_dim(rel_pos, lax.axis_index(HEAD) * rows, rows, 0)
    own_stats = score_stats(rel_pos, mla_query, latent_keys, lax.axis_size(KEY))
    all_stats = exchanged(own_stats, KEY)
    logits, row_stat = index_logits(row_pos, index_query, index_weights, index_keys)
    share = head_share(all_stats, rel_pos, mla_query, latent_keys)
    parts = exchanged(share.reshape(heads_axis, rows, keys), HEAD)
    row_stats = spread(row_stat[:, 0].reshape(1, rows), KEY)
    high = jnp.max(row_stats, axis=0)
    row_total = high + jnp.log2(jnp.sum(jnp.exp2(row_stats - high), axis=0))
    grad_rows, grad_keys = gradients(
        parts, logits, row_total.reshape(rows, 1), index_query, index_weights, index_keys,
        lax.axis_size(KEY) * keys,
    )
    key_grads = summed(grad_keys, HEAD)
    mine = summed(summed(grad_rows, "core"), FAR)
    near = spread(mine, FAR).reshape(-1, mine.shape[-1])
    query_grads = spread(near, "core").reshape(index_query.shape)
    return (query_grads, key_grads)


def solution(mesh):
    finer = Mesh(mesh.devices.reshape(2, 8, 4, 4, 2), ("yl", "z", "x", "yh", "core"))
    return jax.shard_map(
        shards,
        mesh=finer,
        in_specs=(
            P(),
            P(HEAD, None, None),
            P(KEY, None),
            P(HEAD, None, None),
            P(KEY, None),
            P(HEAD, None),
        ),
        out_specs=(P(HEAD, None, None), P(KEY + HEAD, None)),
        check_vma=False,
    )
```

```python
import functools
import math

import jax
import jax.numpy as jnp
from jax import lax
from jax.experimental import pallas as pl
from jax.experimental.pallas import tpu as pltpu
from jax.sharding import Mesh
from jax.sharding import PartitionSpec as P

HEADS = 128
LANES = 128
KEY = ("x", "yh", "core")
HEAD = ("yl", "zh", "zl")
RING = ("zh", "zl")
SIDE = ("x", "core")
LOG2E = math.log2(math.e)
attn_scale = 192.0 ** (-0.5) * LOG2E
index_scale = 128.0 ** (-0.5)
masked_fill = -1e30
NT = (((1,), (1,)), ((), ()))
NN = (((1,), (0,)), ((), ()))
TN = (((0,), (0,)), ((), ()))


def dot(a, b, dims):
    return lax.dot_general(a, b, dims, preferred_element_type=jnp.float32)


def params(semantics=("arbitrary",)):
    return pltpu.CompilerParams(
        dimension_semantics=semantics, vmem_limit_bytes=48 * 1024 * 1024
    )


def score_stats_kernel(pos_ref, q_ref, k_ref, out_ref, rows_ref, col_ref, *, tile):
    head = pl.program_id(0)
    heads = pl.num_programs(0)
    keys = k_ref.shape[1]
    q = jnp.transpose(q_ref[0])
    rows_ref[0] = q
    rows = q.shape[0]
    pos = jnp.broadcast_to(pos_ref[...], (rows, LANES))
    ids = lax.broadcasted_iota(jnp.int32, (rows, LANES), 1)
    highs, sums = [], []
    for start in range(0, keys, tile):
        scores = dot(q, k_ref[:, start : start + tile], NN)
        lines = [
            jnp.where(
                ids + (start + at) <= pos, scores[:, at : at + LANES] * attn_scale, masked_fill
            )
            for at in range(0, tile, LANES)
        ]
        high = functools.reduce(jnp.maximum, lines)
        highs.append(high)
        sums.append(sum(jnp.exp2(line - high) for line in lines))
    high = functools.reduce(jnp.maximum, highs)
    total = sum(s * jnp.exp2(h - high) for h, s in zip(highs, sums))
    most = jnp.max(high, axis=1, keepdims=True)
    total = jnp.sum(total * jnp.exp2(high - most), axis=1, keepdims=True)
    line = most + jnp.log2(total)
    col_ref[...] = jnp.where(ids == head, line, col_ref[...])

    @pl.when(head == heads - 1)
    def _():
        for at in range(0, rows, LANES):
            out_ref[at // LANES] = jnp.transpose(col_ref[at : at + LANES, :])[: out_ref.shape[1], :]


def score_stats(rel_pos, q, k):
    heads, width, rows = q.shape
    keys = k.shape[1]
    return pl.pallas_call(
        functools.partial(score_stats_kernel, tile=512),
        grid=(heads,),
        in_specs=[
            pl.BlockSpec((rows, 1), lambda h: (0, 0)),
            pl.BlockSpec((1, width, rows), lambda h: (h, 0, 0)),
            pl.BlockSpec((width, keys), lambda h: (0, 0)),
        ],
        out_specs=(
            pl.BlockSpec((rows // LANES, heads, LANES), lambda h: (0, 0, 0)),
            pl.BlockSpec((1, rows, width), lambda h: (h, 0, 0)),
        ),
        out_shape=(
            jax.ShapeDtypeStruct((rows // LANES, heads, LANES), jnp.float32),
            jax.ShapeDtypeStruct((heads, rows, width), q.dtype),
        ),
        scratch_shapes=[pltpu.VMEM((rows, LANES), jnp.float32)],
        compiler_params=params(),
        cost_estimate=pl.CostEstimate(
            flops=2 * heads * rows * keys * width, transcendentals=heads * rows * keys, bytes_accessed=6 << 20
        ),
        name="score_stats",
    )(rel_pos.reshape(rows, 1), q, k)


def combined(stats):
    high = jnp.max(stats, axis=0)
    return high + jnp.log2(jnp.sum(jnp.exp2(stats - high[None]), axis=0))


def head_share_kernel(half_ref, stats_ref, pos_ref, q_ref, k_ref, out_ref, col_ref):
    heads, rows, _ = q_ref.shape
    tile = k_ref.shape[1]
    step = pl.program_id(0)

    @pl.when(step == 0)
    def _():
        line = combined(stats_ref[...]) + math.log2(HEADS)
        lines = [line[:, head * rows : (head + 1) * rows] for head in range(heads)]
        col_ref[:, :heads] = jnp.transpose(jnp.concatenate(lines, axis=0))

    k = k_ref[...]
    total = None
    for head in range(heads):
        scores = dot(q_ref[head], k, NN)
        part = jnp.exp2(scores * attn_scale - col_ref[:, head : head + 1])
        total = part if total is None else total + part
    start = (half_ref[1] * pl.num_programs(0) + step) * tile
    ids = lax.broadcasted_iota(jnp.int32, total.shape, 1) + start
    out_ref[...] = jnp.where(ids <= pos_ref[...], total, 0.0)


def head_share(half, stats, rel_pos, q, k):
    heads, rows, width = q.shape
    rows //= 2
    keys = k.shape[1] // 2
    tile = 256
    steps = keys // tile
    return pl.pallas_call(
        head_share_kernel,
        grid_spec=pltpu.PrefetchScalarGridSpec(
            num_scalar_prefetch=1,
            grid=(steps,),
            in_specs=[
                pl.BlockSpec((stats.shape[0], 1, heads * rows), lambda t, half: (0, 0, half[0])),
                pl.BlockSpec((rows, 1), lambda t, half: (half[0], 0)),
                pl.BlockSpec((heads, rows, width), lambda t, half: (0, half[0], 0)),
                pl.BlockSpec((width, tile), lambda t, half: (0, half[1] * steps + t)),
            ],
            out_specs=pl.BlockSpec((rows, tile), lambda t, half: (0, t)),
            scratch_shapes=[pltpu.VMEM((rows, LANES), jnp.float32)],
        ),
        out_shape=jax.ShapeDtypeStruct((rows, keys), jnp.float32),
        compiler_params=params(),
        cost_estimate=pl.CostEstimate(
            flops=2 * heads * rows * keys * width, transcendentals=heads * rows * keys, bytes_accessed=3 << 20
        ),
        name="head_share",
    )(half, stats, rel_pos.reshape(2 * rows, 1), q, k)


def diagonal(rows):
    shape = (rows, LANES)
    return lax.broadcasted_iota(jnp.int32, shape, 0) == lax.broadcasted_iota(jnp.int32, shape, 1)


def index_logits_kernel(pos_ref, q_ref, w_ref, k_ref, own_ref, logit_ref, stat_ref):
    rows = pos_ref.shape[0]
    iheads = q_ref.shape[0] // rows
    keys = k_ref.shape[0]
    tile = 512
    w = jnp.transpose(w_ref[...])
    for start in range(0, keys, tile):
        k = k_ref[start : start + tile, :]
        lines = []
        for row in range(rows):
            own = slice(row * iheads, (row + 1) * iheads)
            dots = dot(q_ref[own, :], k, NT)
            lines.append(
                jnp.sum(jnp.maximum(dots, 0.0) * w[:, row : row + 1], axis=0, keepdims=True)
            )
        logits = jnp.concatenate(lines, axis=0) * (index_scale * LOG2E)
        ids = lax.broadcasted_iota(jnp.int32, logits.shape, 1) + start
        logit_ref[:, start : start + tile] = jnp.where(ids <= pos_ref[...], logits, masked_fill)
    logits = logit_ref[...]
    high = jnp.max(logits, axis=1, keepdims=True)
    total = jnp.sum(jnp.exp2(logits - high), axis=1, keepdims=True)
    line = jnp.where(diagonal(rows), high + jnp.log2(total), 0.0)
    line = jnp.sum(line, axis=0, keepdims=True)
    groups, heads, _ = own_ref.shape
    copies = stat_ref.shape[0]
    lines = [own_ref[group, head : head + 1, :] for group in range(groups) for head in range(heads)]
    for at, part in enumerate(lines + [line]):
        stat_ref[:, :, at * LANES : (at + 1) * LANES] = jnp.broadcast_to(
            part[None], (copies, 1, LANES)
        )


def index_logits(row_pos, q, w, k, own, copies):
    rows, iheads, width = q.shape
    keys = k.shape[0]
    return pl.pallas_call(
        index_logits_kernel,
        out_shape=(
            jax.ShapeDtypeStruct((rows, keys), jnp.float32),
            jax.ShapeDtypeStruct((copies, 1, own.size + LANES), jnp.float32),
        ),
        compiler_params=pltpu.CompilerParams(vmem_limit_bytes=48 * 1024 * 1024),
        cost_estimate=pl.CostEstimate(
            flops=2 * rows * iheads * keys * width, transcendentals=rows * keys, bytes_accessed=1 << 20
        ),
        name="index_logits",
    )(row_pos.reshape(rows, 1), q.reshape(rows * iheads, width), w, k, own)


def gradients_kernel(
    half_ref, parts_ref, logit_ref, stat_ref, q_ref, w_ref, k_ref, before_ref, rows_ref, keys_ref, total_ref, w_col_ref, *, count
):
    step = pl.program_id(0)
    rows = logit_ref.shape[0]
    iheads = q_ref.shape[0] // rows

    @pl.when(step == 0)
    def _():
        line = combined(stat_ref[...])
        total_ref[...] = jnp.sum(jnp.where(diagonal(rows), line, 0.0), axis=1, keepdims=True)
        w_col_ref[...] = jnp.transpose(w_ref[...])

    target = jnp.sum(parts_ref[...], axis=0)
    probs = jnp.exp2(logit_ref[...] - total_ref[...])
    slope = (probs - target) * count
    k = k_ref[...]
    w = w_col_ref[...]
    coefs = []
    for row in range(rows):
        own = slice(row * iheads, (row + 1) * iheads)
        dots = dot(q_ref[own, :], k, NT)
        coef = jnp.where(dots > 0, slope[row : row + 1, :] * w[:, row : row + 1] * index_scale, 0.0)
        coefs.append(coef.astype(jnp.bfloat16))
    coef = jnp.concatenate(coefs, axis=0)
    grad_keys = dot(coef, q_ref[...], TN)
    near, far, share, _ = keys_ref.shape
    for other in range(far):
        for side in range(near):
            at = (other * near + side) * share
            keys_ref[side, other] = grad_keys[at : at + share, :]
    part = dot(coef, k, NN)

    @pl.when(step == 0)
    def _():
        rows_ref[...] = part if before_ref is None else before_ref[...] + part

    @pl.when(step > 0)
    def _():
        rows_ref[...] += part


def gradients(half, parts, logits, stats, q, w, k, before, count, sizes):
    rows, iheads, width = q.shape
    keys = parts.shape[2]
    flat = rows * iheads
    _, nf, nz = sizes
    share = keys // (nf * nz)
    far = nf // 2
    tile = far * nz * share
    last = stats.shape[2] // LANES - 1
    body = gradients_kernel
    operands = [parts, logits, stats, q.reshape(flat, width), w, k]
    in_specs = [
        pl.BlockSpec((parts.shape[0], rows, tile), lambda t, half: (0, 0, t)),
        pl.BlockSpec((rows, tile), lambda t, half: (0, half[0] * 2 + t)),
        pl.BlockSpec((stats.shape[0], 1, LANES), lambda t, half: (0, 0, last)),
        pl.BlockSpec((flat, width), lambda t, half: (0, 0)),
        pl.BlockSpec((rows, iheads), lambda t, half: (0, 0)),
        pl.BlockSpec((tile, width), lambda t, half: (half[0] * 2 + t, 0)),
    ]
    if before is None:
        body = lambda *refs, count: gradients_kernel(*refs[:7], None, *refs[7:], count=count)
    else:
        operands.append(before)
        in_specs.append(pl.BlockSpec((flat, width), lambda t, half: (0, 0)))
    return pl.pallas_call(
        functools.partial(body, count=float(count)),
        grid_spec=pltpu.PrefetchScalarGridSpec(
            num_scalar_prefetch=1,
            grid=(keys // tile,),
            in_specs=in_specs,
            out_specs=(
                pl.BlockSpec((flat, width), lambda t, half: (0, 0)),
                pl.BlockSpec((nz, far, share, width), lambda t, half: (0, t, 0, 0)),
            ),
            scratch_shapes=[pltpu.VMEM((rows, 1), jnp.float32), pltpu.VMEM((iheads, rows), jnp.float32)],
        ),
        out_shape=(
            jax.ShapeDtypeStruct((flat, width), jnp.float32),
            jax.ShapeDtypeStruct((nz, nf, share, width), jnp.float32),
        ),
        compiler_params=params(),
        cost_estimate=pl.CostEstimate(
            flops=6 * flat * keys * width, transcendentals=rows * keys, bytes_accessed=2 << 20
        ),
        name="gradients",
    )(half, *operands)


def exchanged(parts, axis):
    return lax.all_to_all(parts, axis, split_axis=0, concat_axis=0, tiled=True)


def spread(shard, axis):
    size = lax.axis_size(axis)
    return exchanged(jnp.broadcast_to(shard[None], (size, *shard.shape)), axis)


def summed(shard, axis):
    size = lax.axis_size(axis)
    parts = exchanged(shard.reshape(size, -1, shard.shape[-1]), axis)
    return parts.sum(axis=0)


def at_owner(parts, axis):
    size = lax.axis_size(axis)
    own = lax.axis_index(axis)
    total = lax.dynamic_index_in_dim(parts, own, 0, keepdims=False)
    got = []
    for hop in range(1, size):
        part = lax.dynamic_index_in_dim(parts, own ^ hop, 0, keepdims=False)
        got.append(lax.ppermute(part, axis, [(i, i ^ hop) for i in range(size)]))
    return sum(got, total)


def shards(query_pos, mla_query, latent_keys, index_query, index_keys, index_weights):
    keys = latent_keys.shape[0]
    rows = index_query.shape[0]
    rel_pos = query_pos - lax.axis_index(KEY) * keys
    row_pos = lax.dynamic_slice_in_dim(rel_pos, lax.axis_index(HEAD) * rows, rows, 0)
    q = jnp.swapaxes(mla_query, 1, 2)
    k = jnp.swapaxes(latent_keys, 0, 1)
    sizes = [lax.axis_size(axis) for axis in HEAD]
    own_stats, q_rows = score_stats(rel_pos, q, k)
    logits, own_stats = index_logits(
        row_pos, index_query, index_weights, index_keys, own_stats, lax.axis_size(KEY)
    )
    stats = exchanged(own_stats, KEY)
    mine = lax.axis_index("yl")
    other = 1 - mine
    swap = [(0, 1), (1, 0)]

    def pick(*halves):
        return jnp.stack(halves).astype(jnp.int32)

    grad_rows, grad_keys = None, []
    shares = {}
    for name, rows_half, halves in (("sent", other, (mine, other)), ("kept", mine, (other, mine))):
        for turn, half in enumerate(halves):
            shares[name, turn] = head_share(pick(rows_half, half), stats, rel_pos, q_rows, k)
    for turn, half in enumerate((other, mine)):
        near = lax.ppermute(shares["sent", turn], "yl", swap)
        near = (near + shares["kept", turn]).reshape(-1, rows, keys // 2)
        parts = exchanged(near, RING)
        grad_rows, part = gradients(
            pick(half), parts, logits, stats, index_query, index_weights, index_keys, grad_rows,
            lax.axis_size(KEY) * keys, sizes,
        )
        grad_keys.append(part)
    near = lax.ppermute(grad_keys[0], "yl", swap)
    near = near + grad_keys[1]
    near = at_owner(near, "zl")
    key_grads = at_owner(near, "zh")
    total = summed(grad_rows, SIDE)
    total = spread(total, "yh").sum(axis=0)
    query_grads = spread(total, SIDE).reshape(index_query.shape)
    return (query_grads, key_grads)


def solution(mesh):
    finer = Mesh(mesh.devices.reshape(2, 4, 2, 4, 4, 2), HEAD + KEY)
    return jax.shard_map(
        shards,
        mesh=finer,
        in_specs=(
            P(),
            P(HEAD, None, None),
            P(KEY, None),
            P(HEAD, None, None),
            P(KEY, None),
            P(HEAD, None),
        ),
        out_specs=(P(HEAD, None, None), P(KEY + HEAD, None)),
        check_vma=False,
    )
```

```python
import functools
import math

import jax
import jax.numpy as jnp
from jax import lax
from jax.experimental import pallas as pl
from jax.experimental.pallas import tpu as pltpu
from jax.sharding import Mesh
from jax.sharding import PartitionSpec as P

HEADS = 128
LANES = 128
KEY = ("x", "yh", "core")
HEAD = ("yl", "zh", "zl")
RING = ("zh", "zl")
SIDE = ("x", "core")
LOG2E = math.log2(math.e)
attn_scale = 192.0 ** (-0.5) * LOG2E
index_scale = 128.0 ** (-0.5)
masked_fill = -1e30
NT = (((1,), (1,)), ((), ()))
NN = (((1,), (0,)), ((), ()))
TN = (((0,), (0,)), ((), ()))


def in_hbm(x):
    return pltpu.with_memory_space_constraint(x, pltpu.HBM)


def dot(a, b, dims):
    return lax.dot_general(a, b, dims, preferred_element_type=jnp.float32)


def params(semantics=("arbitrary",)):
    return pltpu.CompilerParams(
        dimension_semantics=semantics, vmem_limit_bytes=48 * 1024 * 1024
    )


def score_stats_kernel(pos_ref, q_ref, k_ref, out_ref, rows_ref, col_ref, *, tile):
    head = pl.program_id(0)
    heads = pl.num_programs(0)
    keys = k_ref.shape[1]
    q = jnp.transpose(q_ref[0])
    rows_ref[0] = q
    rows = q.shape[0]
    pos = jnp.broadcast_to(pos_ref[...], (rows, LANES))
    ids = lax.broadcasted_iota(jnp.int32, (rows, LANES), 1)
    highs, sums = [], []
    for start in range(0, keys, tile):
        scores = dot(q, k_ref[:, start : start + tile], NN)
        lines = [
            jnp.where(
                ids + (start + at) <= pos, scores[:, at : at + LANES] * attn_scale, masked_fill
            )
            for at in range(0, tile, LANES)
        ]
        high = functools.reduce(jnp.maximum, lines)
        highs.append(high)
        sums.append(sum(jnp.exp2(line - high) for line in lines))
    high = functools.reduce(jnp.maximum, highs)
    total = sum(s * jnp.exp2(h - high) for h, s in zip(highs, sums))
    most = jnp.max(high, axis=1, keepdims=True)
    total = jnp.sum(total * jnp.exp2(high - most), axis=1, keepdims=True)
    line = most + jnp.log2(total)
    col_ref[...] = jnp.where(ids == head, line, col_ref[...])

    @pl.when(head == heads - 1)
    def _():
        for at in range(0, rows, LANES):
            out_ref[at // LANES] = jnp.transpose(col_ref[at : at + LANES, :])[: out_ref.shape[1], :]


def score_stats(rel_pos, q, k):
    heads, width, rows = q.shape
    keys = k.shape[1]
    return pl.pallas_call(
        functools.partial(score_stats_kernel, tile=512),
        grid=(heads,),
        in_specs=[
            pl.BlockSpec((rows, 1), lambda h: (0, 0)),
            pl.BlockSpec((1, width, rows), lambda h: (h, 0, 0)),
            pl.BlockSpec((width, keys), lambda h: (0, 0)),
        ],
        out_specs=(
            pl.BlockSpec((rows // LANES, heads, LANES), lambda h: (0, 0, 0)),
            pl.BlockSpec((1, rows, width), lambda h: (h, 0, 0)),
        ),
        out_shape=(
            jax.ShapeDtypeStruct((rows // LANES, heads, LANES), jnp.float32),
            pltpu.HBM((heads, rows, width), q.dtype),
        ),
        scratch_shapes=[pltpu.VMEM((rows, LANES), jnp.float32)],
        compiler_params=params(),
        cost_estimate=pl.CostEstimate(
            flops=2 * heads * rows * keys * width, transcendentals=heads * rows * keys, bytes_accessed=6 << 20
        ),
        name="score_stats",
    )(rel_pos.reshape(rows, 1), in_hbm(q), k)


def combined(stats):
    high = jnp.max(stats, axis=0)
    return high + jnp.log2(jnp.sum(jnp.exp2(stats - high[None]), axis=0))


def head_share_kernel(half_ref, stats_ref, pos_ref, q_ref, k_ref, out_ref, col_ref):
    heads, rows, _ = q_ref.shape
    tile = k_ref.shape[1]
    step = pl.program_id(0)

    @pl.when(step == 0)
    def _():
        line = combined(stats_ref[...]) + math.log2(HEADS)
        lines = [line[:, head * rows : (head + 1) * rows] for head in range(heads)]
        col_ref[:, :heads] = jnp.transpose(jnp.concatenate(lines, axis=0))

    k = k_ref[...]
    total = None
    for head in range(heads):
        scores = dot(q_ref[head], k, NN)
        part = jnp.exp2(scores * attn_scale - col_ref[:, head : head + 1])
        total = part if total is None else total + part
    start = (half_ref[1] * pl.num_programs(0) + step) * tile
    ids = lax.broadcasted_iota(jnp.int32, total.shape, 1) + start
    out_ref[...] = jnp.where(ids <= pos_ref[...], total, 0.0)


def head_share(half, stats, rel_pos, q, k):
    heads, rows, width = q.shape
    rows //= 2
    keys = k.shape[1] // 2
    tile = 256
    steps = keys // tile
    return pl.pallas_call(
        head_share_kernel,
        grid_spec=pltpu.PrefetchScalarGridSpec(
            num_scalar_prefetch=1,
            grid=(steps,),
            in_specs=[
                pl.BlockSpec((stats.shape[0], 1, heads * rows), lambda t, half: (0, 0, half[0])),
                pl.BlockSpec((rows, 1), lambda t, half: (half[0], 0)),
                pl.BlockSpec((heads, rows, width), lambda t, half: (0, half[0], 0)),
                pl.BlockSpec((width, tile), lambda t, half: (0, half[1] * steps + t)),
            ],
            out_specs=pl.BlockSpec((rows, tile), lambda t, half: (0, t)),
            scratch_shapes=[pltpu.VMEM((rows, LANES), jnp.float32)],
        ),
        out_shape=jax.ShapeDtypeStruct((rows, keys), jnp.float32),
        compiler_params=params(),
        cost_estimate=pl.CostEstimate(
            flops=2 * heads * rows * keys * width, transcendentals=heads * rows * keys, bytes_accessed=3 << 20
        ),
        name="head_share",
    )(half, stats, rel_pos.reshape(2 * rows, 1), in_hbm(q), k)


def diagonal(rows):
    shape = (rows, LANES)
    return lax.broadcasted_iota(jnp.int32, shape, 0) == lax.broadcasted_iota(jnp.int32, shape, 1)


def index_logits_kernel(pos_ref, q_ref, w_ref, k_ref, own_ref, logit_ref, stat_ref):
    rows = pos_ref.shape[0]
    iheads = q_ref.shape[0] // rows
    keys = k_ref.shape[0]
    tile = 512
    w = jnp.transpose(w_ref[...])
    for start in range(0, keys, tile):
        k = k_ref[start : start + tile, :]
        lines = []
        dots = jnp.maximum(dot(q_ref[...], k, NT), 0.0)
        for row in range(rows):
            own = dots[row * iheads : (row + 1) * iheads, :]
            lines.append(jnp.sum(own * w[:, row : row + 1], axis=0, keepdims=True))
        logits = jnp.concatenate(lines, axis=0) * (index_scale * LOG2E)
        ids = lax.broadcasted_iota(jnp.int32, logits.shape, 1) + start
        logit_ref[:, start : start + tile] = jnp.where(ids <= pos_ref[...], logits, masked_fill)
    logits = logit_ref[...]
    high = jnp.max(logits, axis=1, keepdims=True)
    total = jnp.sum(jnp.exp2(logits - high), axis=1, keepdims=True)
    line = jnp.where(diagonal(rows), high + jnp.log2(total), 0.0)
    line = jnp.sum(line, axis=0, keepdims=True)
    groups, heads, _ = own_ref.shape
    copies = stat_ref.shape[0]
    lines = [own_ref[group, head : head + 1, :] for group in range(groups) for head in range(heads)]
    for at, part in enumerate(lines + [line]):
        stat_ref[:, :, at * LANES : (at + 1) * LANES] = jnp.broadcast_to(
            part[None], (copies, 1, LANES)
        )


def index_logits(row_pos, q, w, k, own, copies):
    rows, iheads, width = q.shape
    keys = k.shape[0]
    return pl.pallas_call(
        index_logits_kernel,
        out_shape=(
            pltpu.HBM((rows, keys), jnp.float32),
            pltpu.HBM((copies, 1, own.size + LANES), jnp.float32),
        ),
        compiler_params=pltpu.CompilerParams(vmem_limit_bytes=48 * 1024 * 1024),
        cost_estimate=pl.CostEstimate(
            flops=2 * rows * iheads * keys * width, transcendentals=rows * keys, bytes_accessed=1 << 20
        ),
        name="index_logits",
    )(row_pos.reshape(rows, 1), q.reshape(rows * iheads, width), w, k, own)


def gradients_kernel(half_ref, parts_ref, logit_ref, stat_ref, q_ref, w_ref, k_ref, *refs, count, before, row_part, key_part):
    refs = list(refs)
    before_ref = refs.pop(0) if before else None
    rows_ref = refs.pop(0) if row_part else None
    keys_ref = refs.pop(0) if key_part else None
    total_ref, w_col_ref = refs
    step = pl.program_id(0)
    rows = logit_ref.shape[0]
    iheads = q_ref.shape[0] // rows

    @pl.when(step == 0)
    def _():
        line = combined(stat_ref[...])
        total_ref[...] = jnp.sum(jnp.where(diagonal(rows), line, 0.0), axis=1, keepdims=True)
        w_col_ref[...] = jnp.transpose(w_ref[...])

    target = jnp.sum(parts_ref[...], axis=0)
    probs = jnp.exp2(logit_ref[...] - total_ref[...])
    slope = (probs - target) * count
    k = k_ref[...]
    w = w_col_ref[...]
    dots = dot(q_ref[...], k, NT)
    coefs = []
    for row in range(rows):
        own = dots[row * iheads : (row + 1) * iheads, :]
        coef = jnp.where(own > 0, slope[row : row + 1, :] * w[:, row : row + 1] * index_scale, 0.0)
        coefs.append(coef.astype(jnp.bfloat16))
    coef = jnp.concatenate(coefs, axis=0)
    if key_part:
        grad_keys = dot(coef, q_ref[...], TN)
        near, far, share, _ = keys_ref.shape
        for other in range(far):
            for side in range(near):
                at = (other * near + side) * share
                keys_ref[side, other] = grad_keys[at : at + share, :]
    if row_part:
        part = dot(coef, k, NN)

        @pl.when(step == 0)
        def _():
            rows_ref[...] = before_ref[...] + part if before else part

        @pl.when(step > 0)
        def _():
            rows_ref[...] += part


def gradients(half, parts, logits, stats, q, w, k, before, count, sizes, row_part, key_part):
    rows, iheads, width = q.shape
    keys = parts.shape[2]
    flat = rows * iheads
    _, nf, nz = sizes
    share = keys // (nf * nz)
    far = nf // 2
    tile = far * nz * share
    last = stats.shape[2] // LANES - 1
    operands = [parts, logits, stats, q.reshape(flat, width), w, k]
    in_specs = [
        pl.BlockSpec((parts.shape[0], rows, tile), lambda t, half: (0, 0, t)),
        pl.BlockSpec((rows, tile), lambda t, half: (0, half[0] * 2 + t)),
        pl.BlockSpec((stats.shape[0], 1, LANES), lambda t, half: (0, 0, last)),
        pl.BlockSpec((flat, width), lambda t, half: (0, 0)),
        pl.BlockSpec((rows, iheads), lambda t, half: (0, 0)),
        pl.BlockSpec((tile, width), lambda t, half: (half[0] * 2 + t, 0)),
    ]
    row_spec = pl.BlockSpec((flat, width), lambda t, half: (0, 0))
    if before is not None:
        operands.append(before)
        in_specs.append(row_spec)
    out_specs, out_shape = [], []
    if row_part:
        out_specs.append(row_spec)
        out_shape.append(jax.ShapeDtypeStruct((flat, width), jnp.float32))
    if key_part:
        out_specs.append(pl.BlockSpec((nz, far, share, width), lambda t, half: (0, t, 0, 0)))
        out_shape.append(jax.ShapeDtypeStruct((nz, nf, share, width), jnp.float32))
    return pl.pallas_call(
        functools.partial(
            gradients_kernel, count=float(count), before=before is not None, row_part=row_part, key_part=key_part
        ),
        grid_spec=pltpu.PrefetchScalarGridSpec(
            num_scalar_prefetch=1,
            grid=(keys // tile,),
            in_specs=in_specs,
            out_specs=out_specs,
            scratch_shapes=[pltpu.VMEM((rows, 1), jnp.float32), pltpu.VMEM((iheads, rows), jnp.float32)],
        ),
        out_shape=out_shape,
        compiler_params=params(),
        cost_estimate=pl.CostEstimate(
            flops=(2 + 2 * row_part + 2 * key_part) * flat * keys * width,
            transcendentals=rows * keys,
            bytes_accessed=2 << 20,
        ),
        name="gradients",
    )(half, parts, in_hbm(logits), *operands[2:])


def sum_copies_kernel(parts_ref, out_ref):
    total = jnp.sum(parts_ref[...], axis=0)
    out_ref[...] = jnp.broadcast_to(total[None], out_ref.shape)


def sum_copies(parts, copies):
    return pl.pallas_call(
        sum_copies_kernel,
        out_shape=jax.ShapeDtypeStruct((copies, *parts.shape[1:]), parts.dtype),
        compiler_params=pltpu.CompilerParams(vmem_limit_bytes=8 * 1024 * 1024),
        name="sum_copies",
    )(parts)


def exchanged(parts, axis):
    return lax.all_to_all(parts, axis, split_axis=0, concat_axis=0, tiled=True)


def at_owner(parts, axis):
    size = lax.axis_size(axis)
    own = lax.axis_index(axis)
    total = lax.dynamic_index_in_dim(parts, own, 0, keepdims=False)
    got = []
    for hop in range(1, size):
        part = lax.dynamic_index_in_dim(parts, own ^ hop, 0, keepdims=False)
        got.append(lax.ppermute(part, axis, [(i, i ^ hop) for i in range(size)]))
    return sum(got, total)


def shards(query_pos, mla_query, latent_keys, index_query, index_keys, index_weights):
    keys = latent_keys.shape[0]
    rows = index_query.shape[0]
    rel_pos = query_pos - lax.axis_index(KEY) * keys
    row_pos = lax.dynamic_slice_in_dim(rel_pos, lax.axis_index(HEAD) * rows, rows, 0)
    q = jnp.swapaxes(mla_query, 1, 2)
    k = jnp.swapaxes(latent_keys, 0, 1)
    sizes = [lax.axis_size(axis) for axis in HEAD]
    own_stats, q_rows = score_stats(rel_pos, q, k)
    logits, own_stats = index_logits(
        row_pos, index_query, index_weights, index_keys, own_stats, lax.axis_size(KEY)
    )
    stats = exchanged(own_stats, KEY)
    mine = lax.axis_index("yl")
    other = 1 - mine
    swap = [(0, 1), (1, 0)]

    def pick(*halves):
        return jnp.stack(halves).astype(jnp.int32)

    grad_rows, grad_keys = None, []
    shares = {}
    for name, rows_half, halves in (("sent", other, (mine, other)), ("kept", mine, (other, mine))):
        for turn, half in enumerate(halves):
            shares[name, turn] = head_share(pick(rows_half, half), stats, rel_pos, q_rows, k)
    for turn, half in enumerate((other, mine)):
        near = lax.ppermute(shares["sent", turn], "yl", swap)
        near = (near + shares["kept", turn]).reshape(-1, rows, keys // 2)
        parts = exchanged(near, RING)

        def grads(rows_before, row_part, key_part):
            return gradients(
                pick(half), parts, logits, stats, index_query, index_weights, index_keys, rows_before,
                lax.axis_size(KEY) * keys, sizes, row_part, key_part,
            )

        if turn == 0:
            grad_rows, part = grads(None, True, True)
        else:
            (grad_rows,) = grads(grad_rows, True, False)
        if turn == 1:
            (part,) = grads(None, False, True)
        grad_keys.append(part)
    near = lax.ppermute(grad_keys[0], "yl", swap)
    near = near + grad_keys[1]
    near = at_owner(near, "zl")
    key_grads = at_owner(near, "zh")
    side = lax.axis_size(SIDE)
    total = exchanged(grad_rows.reshape(side, -1, grad_rows.shape[1]), SIDE)
    total = exchanged(sum_copies(total, lax.axis_size("yh")), "yh")
    query_grads = exchanged(sum_copies(total, side), SIDE).reshape(index_query.shape)
    return (query_grads, key_grads)


def solution(mesh):
    finer = Mesh(mesh.devices.reshape(2, 4, 2, 4, 4, 2), HEAD + KEY)
    return jax.shard_map(
        shards,
        mesh=finer,
        in_specs=(
            P(),
            P(HEAD, None, None),
            P(KEY, None),
            P(HEAD, None, None),
            P(KEY, None),
            P(HEAD, None),
        ),
        out_specs=(P(HEAD, None, None), P(KEY + HEAD, None)),
        check_vma=False,
    )
```

```python
import functools
import math

import jax
import jax.numpy as jnp
from jax import lax
from jax.experimental import pallas as pl
from jax.experimental.pallas import tpu as pltpu
from jax.sharding import Mesh
from jax.sharding import PartitionSpec as P

HEADS = 128
LANES = 128
PIECE = 144
TILE = 512
KEY = ("x", "yh", "core")
HEAD = ("yl", "zh", "zl")
RING = ("zh", "zl")
SIDE = ("x", "core")
LOG2E = math.log2(math.e)
attn_scale = 192.0 ** (-0.5) * LOG2E
index_scale = 128.0 ** (-0.5)
masked_fill = -1e30
NT = (((1,), (1,)), ((), ()))
NN = (((1,), (0,)), ((), ()))
TN = (((0,), (0,)), ((), ()))


def in_hbm(x):
    return pltpu.with_memory_space_constraint(x, pltpu.HBM)


def in_vmem(x):
    return pltpu.with_memory_space_constraint(x, pltpu.VMEM)


def dot(a, b, dims):
    return lax.dot_general(a, b, dims, preferred_element_type=jnp.float32)


def params(mebibytes=24):
    return pltpu.CompilerParams(
        dimension_semantics=("arbitrary",), vmem_limit_bytes=mebibytes * 1024 * 1024
    )


def score_stats_kernel(pos_ref, q_ref, source_ref, out_ref, rows_ref, k_ref, col_ref, sems, *, tile):
    head = pl.program_id(0)
    heads = pl.num_programs(0)
    keys = k_ref.shape[1]
    copies = [
        pltpu.make_async_copy(
            source_ref.at[pl.ds(at * PIECE, PIECE), :], k_ref.at[pl.ds(at * PIECE, PIECE), :], sems.at[at]
        )
        for at in range(k_ref.shape[0] // PIECE)
    ]

    @pl.when(head == 0)
    def _():
        for copy in copies:
            copy.start()
        for copy in copies:
            copy.wait()

    q = jnp.transpose(q_ref[0])
    rows_ref[0] = q
    rows = q.shape[0]
    pos = jnp.broadcast_to(pos_ref[...], (rows, LANES))
    ids = lax.broadcasted_iota(jnp.int32, (rows, LANES), 1)
    highs, sums = [], []
    for start in range(0, keys, tile):
        scores = dot(q, k_ref[:, start : start + tile], NN)
        lines = [
            jnp.where(
                ids + (start + at) <= pos, scores[:, at : at + LANES] * attn_scale, masked_fill
            )
            for at in range(0, tile, LANES)
        ]
        high = functools.reduce(jnp.maximum, lines)
        highs.append(high)
        sums.append(sum(jnp.exp2(line - high) for line in lines))
    high = functools.reduce(jnp.maximum, highs)
    total = sum(s * jnp.exp2(h - high) for h, s in zip(highs, sums))
    most = jnp.max(high, axis=1, keepdims=True)
    total = jnp.sum(total * jnp.exp2(high - most), axis=1, keepdims=True)
    line = most + jnp.log2(total)
    col_ref[...] = jnp.where(ids == head, line, col_ref[...])

    @pl.when(head == heads - 1)
    def _():
        for at in range(0, rows, LANES):
            out_ref[at // LANES] = jnp.transpose(col_ref[at : at + LANES, :])[: out_ref.shape[1], :]


def score_stats(rel_pos, q, k):
    heads, width, rows = q.shape
    keys = k.shape[1]
    return pl.pallas_call(
        functools.partial(score_stats_kernel, tile=512),
        grid=(heads,),
        in_specs=[
            pl.BlockSpec((rows, 1), lambda h: (0, 0)),
            pl.BlockSpec((1, width, rows), lambda h: (h, 0, 0)),
            pl.BlockSpec(memory_space=pl.ANY),
        ],
        out_specs=(
            pl.BlockSpec((rows // LANES, heads, LANES), lambda h: (0, 0, 0)),
            pl.BlockSpec((1, rows, width), lambda h: (h, 0, 0)),
            pl.BlockSpec(memory_space=pltpu.VMEM),
        ),
        out_shape=(
            jax.ShapeDtypeStruct((rows // LANES, heads, LANES), jnp.float32),
            pltpu.HBM((heads, rows, width), q.dtype),
            pltpu.VMEM((width, keys), k.dtype),
        ),
        scratch_shapes=[
            pltpu.VMEM((rows, LANES), jnp.float32),
            pltpu.SemaphoreType.DMA((width // PIECE,)),
        ],
        compiler_params=params(),
        cost_estimate=pl.CostEstimate(
            flops=2 * heads * rows * keys * width, transcendentals=heads * rows * keys, bytes_accessed=6 << 20
        ),
        name="score_stats",
    )(rel_pos.reshape(rows, 1), in_hbm(q), in_hbm(k))


def combined(stats):
    high = jnp.max(stats, axis=0)
    return high + jnp.log2(jnp.sum(jnp.exp2(stats - high[None]), axis=0))


def head_share_kernel(mine_ref, stats_ref, pos_ref, q_ref, k_ref, out_ref, col_ref, *, other_keys):
    head = pl.program_id(0)
    heads = pl.num_programs(0)
    rows, keys = out_ref.shape

    @pl.when(head == 0)
    def _():
        line = combined(stats_ref[...]) + math.log2(HEADS)
        lines = [line[:, at * rows : (at + 1) * rows] for at in range(col_ref.shape[0])]
        cols = jnp.transpose(jnp.concatenate(lines, axis=0))
        for at in range(col_ref.shape[0]):
            col_ref[at] = jnp.broadcast_to(cols[:, at : at + 1], col_ref.shape[1:])
        out_ref[...] = jnp.zeros(out_ref.shape, jnp.float32)

    half = 1 - mine_ref[0] if other_keys else mine_ref[0]
    start = pl.multiple_of(half * keys, keys)
    q = q_ref[0]
    line = col_ref[head]
    for at in range(0, keys, TILE):
        scores = dot(q, k_ref[:, pl.ds(start + at, TILE)], NN) * attn_scale
        for lane in range(0, TILE, LANES):
            out_ref[:, at + lane : at + lane + LANES] += jnp.exp2(
                scores[:, lane : lane + LANES] - line
            )

    @pl.when(head == heads - 1)
    def _():
        ids = lax.broadcasted_iota(jnp.int32, out_ref.shape, 1) + start
        out_ref[...] = jnp.where(ids <= pos_ref[...], out_ref[...], 0.0)


def head_share(mine, other_rows, other_keys, stats, rel_pos, q, k):
    heads, rows, width = q.shape
    rows //= 2
    keys = k.shape[1] // 2

    def part(mine):
        return 1 - mine[0] if other_rows else mine[0]

    return pl.pallas_call(
        functools.partial(head_share_kernel, other_keys=other_keys),
        grid_spec=pltpu.PrefetchScalarGridSpec(
            num_scalar_prefetch=1,
            grid=(heads,),
            in_specs=[
                pl.BlockSpec((stats.shape[0], 1, heads * rows), lambda h, mine: (0, 0, part(mine))),
                pl.BlockSpec((rows, 1), lambda h, mine: (part(mine), 0)),
                pl.BlockSpec((1, rows, width), lambda h, mine: (h, part(mine), 0)),
                pl.BlockSpec(memory_space=pltpu.VMEM),
            ],
            out_specs=pl.BlockSpec((rows, keys), lambda h, mine: (0, 0)),
            scratch_shapes=[pltpu.VMEM((heads, rows, LANES), jnp.float32)],
        ),
        out_shape=jax.ShapeDtypeStruct((rows, keys), jnp.float32),
        compiler_params=params(12),
        cost_estimate=pl.CostEstimate(
            flops=2 * heads * rows * keys * width, transcendentals=heads * rows * keys, bytes_accessed=3 << 20
        ),
        name="head_share",
    )(mine, stats, rel_pos.reshape(2 * rows, 1), in_hbm(q), in_vmem(k))


def diagonal(rows):
    shape = (rows, LANES)
    return lax.broadcasted_iota(jnp.int32, shape, 0) == lax.broadcasted_iota(jnp.int32, shape, 1)


def index_logits_kernel(pos_ref, q_ref, w_ref, k_ref, own_ref, logit_ref, stat_ref):
    rows = pos_ref.shape[0]
    iheads = q_ref.shape[0] // rows
    keys = k_ref.shape[0]
    tile = 512
    w = jnp.transpose(w_ref[...])
    for start in range(0, keys, tile):
        k = k_ref[start : start + tile, :]
        lines = []
        dots = jnp.maximum(dot(q_ref[...], k, NT), 0.0)
        for row in range(rows):
            own = dots[row * iheads : (row + 1) * iheads, :]
            lines.append(jnp.sum(own * w[:, row : row + 1], axis=0, keepdims=True))
        logits = jnp.concatenate(lines, axis=0) * (index_scale * LOG2E)
        ids = lax.broadcasted_iota(jnp.int32, logits.shape, 1) + start
        logit_ref[:, start : start + tile] = jnp.where(ids <= pos_ref[...], logits, masked_fill)
    logits = logit_ref[...]
    high = jnp.max(logits, axis=1, keepdims=True)
    total = jnp.sum(jnp.exp2(logits - high), axis=1, keepdims=True)
    line = jnp.where(diagonal(rows), high + jnp.log2(total), 0.0)
    line = jnp.sum(line, axis=0, keepdims=True)
    groups, heads, _ = own_ref.shape
    copies = stat_ref.shape[0]
    lines = [own_ref[group, head : head + 1, :] for group in range(groups) for head in range(heads)]
    for at, part in enumerate(lines + [line]):
        stat_ref[:, :, at * LANES : (at + 1) * LANES] = jnp.broadcast_to(
            part[None], (copies, 1, LANES)
        )


def index_logits(row_pos, q, w, k, own, copies):
    rows, iheads, width = q.shape
    keys = k.shape[0]
    return pl.pallas_call(
        index_logits_kernel,
        out_shape=(
            pltpu.HBM((rows, keys), jnp.float32),
            pltpu.HBM((copies, 1, own.size + LANES), jnp.float32),
        ),
        compiler_params=pltpu.CompilerParams(vmem_limit_bytes=16 * 1024 * 1024),
        cost_estimate=pl.CostEstimate(
            flops=2 * rows * iheads * keys * width, transcendentals=rows * keys, bytes_accessed=1 << 20
        ),
        name="index_logits",
    )(row_pos.reshape(rows, 1), q.reshape(rows * iheads, width), w, k, own)


def gradients_kernel(half_ref, parts_ref, logit_ref, stat_ref, q_ref, w_ref, k_ref, *refs, count, before, row_part, key_part):
    refs = list(refs)
    before_ref = refs.pop(0) if before else None
    rows_ref = refs.pop(0) if row_part else None
    keys_ref = refs.pop(0) if key_part else None
    total_ref, w_col_ref = refs
    step = pl.program_id(0)
    rows = logit_ref.shape[0]
    iheads = q_ref.shape[0] // rows

    @pl.when(step == 0)
    def _():
        line = combined(stat_ref[...])
        total_ref[...] = jnp.sum(jnp.where(diagonal(rows), line, 0.0), axis=1, keepdims=True)
        w_col_ref[...] = jnp.transpose(w_ref[...])

    target = jnp.sum(parts_ref[...], axis=0)
    probs = jnp.exp2(logit_ref[...] - total_ref[...])
    slope = (probs - target) * count
    k = k_ref[...]
    w = w_col_ref[...]
    dots = dot(q_ref[...], k, NT)
    coefs = []
    for row in range(rows):
        own = dots[row * iheads : (row + 1) * iheads, :]
        coef = jnp.where(own > 0, slope[row : row + 1, :] * w[:, row : row + 1] * index_scale, 0.0)
        coefs.append(coef.astype(jnp.bfloat16))
    coef = jnp.concatenate(coefs, axis=0)
    if key_part:
        grad_keys = dot(coef, q_ref[...], TN)
        near, far, share, _ = keys_ref.shape
        for other in range(far):
            for side in range(near):
                at = (other * near + side) * share
                keys_ref[side, other] = grad_keys[at : at + share, :]
    if row_part:
        part = dot(coef, k, NN)

        @pl.when(step == 0)
        def _():
            rows_ref[...] = before_ref[...] + part if before else part

        @pl.when(step > 0)
        def _():
            rows_ref[...] += part


def gradients(mine, other_keys, parts, logits, stats, q, w, k, before, count, sizes, row_part, key_part):
    rows, iheads, width = q.shape
    keys = parts.shape[2]
    flat = rows * iheads
    _, nf, nz = sizes
    share = keys // (nf * nz)
    far = nf // 2
    tile = far * nz * share
    last = stats.shape[2] // LANES - 1

    def part(mine):
        return 1 - mine[0] if other_keys else mine[0]

    operands = [parts, logits, stats, q.reshape(flat, width), w, k]
    in_specs = [
        pl.BlockSpec((parts.shape[0], rows, tile), lambda t, half: (0, 0, t)),
        pl.BlockSpec((rows, tile), lambda t, mine: (0, part(mine) * 2 + t)),
        pl.BlockSpec((stats.shape[0], 1, LANES), lambda t, half: (0, 0, last)),
        pl.BlockSpec((flat, width), lambda t, half: (0, 0)),
        pl.BlockSpec((rows, iheads), lambda t, half: (0, 0)),
        pl.BlockSpec((tile, width), lambda t, mine: (part(mine) * 2 + t, 0)),
    ]
    row_spec = pl.BlockSpec((flat, width), lambda t, half: (0, 0))
    if before is not None:
        operands.append(before)
        in_specs.append(row_spec)
    out_specs, out_shape = [], []
    if row_part:
        out_specs.append(row_spec)
        out_shape.append(jax.ShapeDtypeStruct((flat, width), jnp.float32))
    if key_part:
        out_specs.append(pl.BlockSpec((nz, far, share, width), lambda t, half: (0, t, 0, 0)))
        out_shape.append(jax.ShapeDtypeStruct((nz, nf, share, width), jnp.float32))
    return pl.pallas_call(
        functools.partial(
            gradients_kernel, count=float(count), before=before is not None, row_part=row_part, key_part=key_part
        ),
        grid_spec=pltpu.PrefetchScalarGridSpec(
            num_scalar_prefetch=1,
            grid=(keys // tile,),
            in_specs=in_specs,
            out_specs=out_specs,
            scratch_shapes=[pltpu.VMEM((rows, 1), jnp.float32), pltpu.VMEM((iheads, rows), jnp.float32)],
        ),
        out_shape=out_shape,
        compiler_params=params(),
        cost_estimate=pl.CostEstimate(
            flops=(2 + 2 * row_part + 2 * key_part) * flat * keys * width,
            transcendentals=rows * keys,
            bytes_accessed=2 << 20,
        ),
        name="gradients",
    )(mine, parts, in_hbm(logits), *operands[2:])


def sum_copies_kernel(parts_ref, out_ref):
    total = jnp.sum(parts_ref[...], axis=0)
    out_ref[...] = jnp.broadcast_to(total[None], out_ref.shape)


def sum_copies(parts, copies):
    return pl.pallas_call(
        sum_copies_kernel,
        out_shape=jax.ShapeDtypeStruct((copies, *parts.shape[1:]), parts.dtype),
        compiler_params=pltpu.CompilerParams(vmem_limit_bytes=8 * 1024 * 1024),
        name="sum_copies",
    )(parts)


def exchanged(parts, axis):
    return lax.all_to_all(parts, axis, split_axis=0, concat_axis=0, tiled=True)


def at_owner(parts, axis):
    size = lax.axis_size(axis)
    own = lax.axis_index(axis)
    total = lax.dynamic_index_in_dim(parts, own, 0, keepdims=False)
    got = []
    for hop in range(1, size):
        part = lax.dynamic_index_in_dim(parts, own ^ hop, 0, keepdims=False)
        got.append(lax.ppermute(part, axis, [(i, i ^ hop) for i in range(size)]))
    return sum(got, total)


def shards(query_pos, mla_query, latent_keys, index_query, index_keys, index_weights):
    keys = latent_keys.shape[0]
    rows = index_query.shape[0]
    rel_pos = query_pos - lax.axis_index(KEY) * keys
    row_pos = lax.dynamic_slice_in_dim(rel_pos, lax.axis_index(HEAD) * rows, rows, 0)
    mine = in_hbm(lax.axis_index("yl").astype(jnp.int32).reshape(1))
    q = jnp.swapaxes(mla_query, 1, 2)
    k = jnp.swapaxes(latent_keys, 0, 1)
    sizes = [lax.axis_size(axis) for axis in HEAD]
    own_stats, q_rows, k_held = score_stats(rel_pos, q, k)
    logits, own_stats = index_logits(
        row_pos, index_query, index_weights, index_keys, own_stats, lax.axis_size(KEY)
    )
    stats = exchanged(own_stats, KEY)
    swap = [(0, 1), (1, 0)]

    grad_rows, grad_keys = None, []
    shares = {}
    for name, first in (("sent", False), ("kept", True)):
        for turn in range(2):
            shares[name, turn] = head_share(mine, name == "sent", first == (turn == 0), stats, rel_pos, q_rows, k_held)
    for turn in range(2):
        near = lax.ppermute(shares["sent", turn], "yl", swap)
        near = (near + shares["kept", turn]).reshape(-1, rows, keys // 2)
        parts = exchanged(near, RING)

        def grads(rows_before, row_part, key_part):
            return gradients(
                mine, turn == 0, parts, logits, stats, index_query, index_weights, index_keys, rows_before,
                lax.axis_size(KEY) * keys, sizes, row_part, key_part,
            )

        if turn == 0:
            grad_rows, part = grads(None, True, True)
        else:
            (grad_rows,) = grads(grad_rows, True, False)
        if turn == 1:
            (part,) = grads(None, False, True)
        grad_keys.append(part)
    near = lax.ppermute(grad_keys[0], "yl", swap)
    near = near + grad_keys[1]
    near = at_owner(near, "zl")
    key_grads = at_owner(near, "zh")
    side = lax.axis_size(SIDE)
    total = exchanged(grad_rows.reshape(side, -1, grad_rows.shape[1]), SIDE)
    total = exchanged(sum_copies(total, lax.axis_size("yh")), "yh")
    query_grads = exchanged(sum_copies(total, side), SIDE).reshape(index_query.shape)
    return (query_grads, key_grads)


def solution(mesh):
    finer = Mesh(mesh.devices.reshape(2, 4, 2, 4, 4, 2), HEAD + KEY)
    return jax.shard_map(
        shards,
        mesh=finer,
        in_specs=(
            P(),
            P(HEAD, None, None),
            P(KEY, None),
            P(HEAD, None, None),
            P(KEY, None),
            P(HEAD, None),
        ),
        out_specs=(P(HEAD, None, None), P(KEY + HEAD, None)),
        check_vma=False,
    )
```

```python
import functools
import math

import jax
import jax.numpy as jnp
from jax import lax
from jax.experimental import pallas as pl
from jax.experimental.pallas import tpu as pltpu
from jax.sharding import Mesh
from jax.sharding import PartitionSpec as P

HEADS = 128
LANES = 128
TILE = 512
KEY = ("x", "yh", "core")
HEAD = ("yl", "zh", "zl")
RING = ("zh", "zl")
SIDE = ("x", "core")
LOG2E = math.log2(math.e)
attn_scale = 192.0 ** (-0.5) * LOG2E
index_scale = 128.0 ** (-0.5)
masked_fill = -1e30
NT = (((1,), (1,)), ((), ()))
NN = (((1,), (0,)), ((), ()))
TN = (((0,), (0,)), ((), ()))


def in_hbm(x):
    return pltpu.with_memory_space_constraint(x, pltpu.HBM)


def in_vmem(x):
    return pltpu.with_memory_space_constraint(x, pltpu.VMEM)


def dot(a, b, dims):
    return lax.dot_general(a, b, dims, preferred_element_type=jnp.float32)


def params(mebibytes=24):
    return pltpu.CompilerParams(
        dimension_semantics=("arbitrary",), vmem_limit_bytes=mebibytes * 1024 * 1024
    )


def score_stats_kernel(pos_ref, q_ref, k_ref, out_ref, rows_ref, col_ref, *, tile):
    head = pl.program_id(0)
    heads = pl.num_programs(0)
    keys = k_ref.shape[1]
    q = jnp.transpose(q_ref[0])
    rows_ref[head] = q
    rows = q.shape[0]
    pos = jnp.broadcast_to(pos_ref[...], (rows, LANES))
    ids = lax.broadcasted_iota(jnp.int32, (rows, LANES), 1)
    highs, sums = [], []
    for start in range(0, keys, tile):
        scores = dot(q, k_ref[:, start : start + tile], NN)
        lines = [
            jnp.where(
                ids + (start + at) <= pos, scores[:, at : at + LANES] * attn_scale, masked_fill
            )
            for at in range(0, tile, LANES)
        ]
        high = functools.reduce(jnp.maximum, lines)
        highs.append(high)
        sums.append(sum(jnp.exp2(line - high) for line in lines))
    high = functools.reduce(jnp.maximum, highs)
    total = sum(s * jnp.exp2(h - high) for h, s in zip(highs, sums))
    most = jnp.max(high, axis=1, keepdims=True)
    total = jnp.sum(total * jnp.exp2(high - most), axis=1, keepdims=True)
    line = most + jnp.log2(total)
    col_ref[...] = jnp.where(ids == head, line, col_ref[...])

    @pl.when(head == heads - 1)
    def _():
        for at in range(0, rows, LANES):
            out_ref[at // LANES] = jnp.transpose(col_ref[at : at + LANES, :])[: out_ref.shape[1], :]


def score_stats(rel_pos, q, k):
    heads, width, rows = q.shape
    keys = k.shape[1]
    return pl.pallas_call(
        functools.partial(score_stats_kernel, tile=512),
        grid=(heads,),
        in_specs=[
            pl.BlockSpec((rows, 1), lambda h: (0, 0)),
            pl.BlockSpec((1, width, rows), lambda h: (h, 0, 0)),
            pl.BlockSpec((width, keys), lambda h: (0, 0)),
        ],
        out_specs=(
            pl.BlockSpec((rows // LANES, heads, LANES), lambda h: (0, 0, 0)),
            pl.BlockSpec(memory_space=pltpu.VMEM),
        ),
        out_shape=(
            jax.ShapeDtypeStruct((rows // LANES, heads, LANES), jnp.float32),
            pltpu.VMEM((heads, rows, width), q.dtype),
        ),
        scratch_shapes=[pltpu.VMEM((rows, LANES), jnp.float32)],
        compiler_params=params(),
        cost_estimate=pl.CostEstimate(
            flops=2 * heads * rows * keys * width, transcendentals=heads * rows * keys, bytes_accessed=6 << 20
        ),
        name="score_stats",
    )(rel_pos.reshape(rows, 1), in_hbm(q), in_hbm(k))


def combined(stats):
    high = jnp.max(stats, axis=0)
    return high + jnp.log2(jnp.sum(jnp.exp2(stats - high[None]), axis=0))


def head_share_kernel(mine_ref, stats_ref, pos_ref, q_ref, k_ref, out_ref, col_ref, *, other_rows, other_keys):
    step = pl.program_id(0)
    heads = q_ref.shape[0]
    rows, tile = out_ref.shape
    mine = mine_ref[0]

    @pl.when(step == 0)
    def _():
        line = combined(stats_ref[...]) + math.log2(HEADS)
        lines = [line[:, head * rows : (head + 1) * rows] for head in range(heads)]
        col_ref[:, :heads] = jnp.transpose(jnp.concatenate(lines, axis=0))

    own = pl.ds(pl.multiple_of((1 - mine if other_rows else mine) * rows, rows), rows)
    k = k_ref[...]
    total = None
    for head in range(heads):
        scores = dot(q_ref[head, own, :], k, NN)
        part = jnp.exp2(scores * attn_scale - col_ref[:, head : head + 1])
        total = part if total is None else total + part
    half = 1 - mine if other_keys else mine
    ids = lax.broadcasted_iota(jnp.int32, total.shape, 1) + (half * pl.num_programs(0) + step) * tile
    out_ref[...] = jnp.where(ids <= pos_ref[...], total, 0.0)


def head_share(mine, other_rows, other_keys, stats, rel_pos, q, k):
    heads, rows, width = q.shape
    rows //= 2
    keys = k.shape[1] // 2
    steps = keys // TILE

    def rows_half(mine):
        return 1 - mine[0] if other_rows else mine[0]

    def keys_half(mine):
        return 1 - mine[0] if other_keys else mine[0]

    return pl.pallas_call(
        functools.partial(head_share_kernel, other_rows=other_rows, other_keys=other_keys),
        grid_spec=pltpu.PrefetchScalarGridSpec(
            num_scalar_prefetch=1,
            grid=(steps,),
            in_specs=[
                pl.BlockSpec((stats.shape[0], 1, heads * rows), lambda t, mine: (0, 0, rows_half(mine))),
                pl.BlockSpec((rows, 1), lambda t, mine: (rows_half(mine), 0)),
                pl.BlockSpec(memory_space=pltpu.VMEM),
                pl.BlockSpec((width, TILE), lambda t, mine: (0, keys_half(mine) * steps + t)),
            ],
            out_specs=pl.BlockSpec((rows, TILE), lambda t, mine: (0, t)),
            scratch_shapes=[pltpu.VMEM((rows, LANES), jnp.float32)],
        ),
        out_shape=jax.ShapeDtypeStruct((rows, keys), jnp.float32),
        compiler_params=params(12),
        cost_estimate=pl.CostEstimate(
            flops=2 * heads * rows * keys * width, transcendentals=heads * rows * keys, bytes_accessed=3 << 20
        ),
        name="head_share",
    )(mine, stats, rel_pos.reshape(2 * rows, 1), in_vmem(q), in_hbm(k))


def diagonal(rows):
    shape = (rows, LANES)
    return lax.broadcasted_iota(jnp.int32, shape, 0) == lax.broadcasted_iota(jnp.int32, shape, 1)


def index_logits_kernel(pos_ref, q_ref, w_ref, k_ref, own_ref, logit_ref, stat_ref):
    rows = pos_ref.shape[0]
    iheads = q_ref.shape[0] // rows
    keys = k_ref.shape[0]
    tile = 512
    w = jnp.transpose(w_ref[...])
    for start in range(0, keys, tile):
        k = k_ref[start : start + tile, :]
        lines = []
        dots = jnp.maximum(dot(q_ref[...], k, NT), 0.0)
        for row in range(rows):
            own = dots[row * iheads : (row + 1) * iheads, :]
            lines.append(jnp.sum(own * w[:, row : row + 1], axis=0, keepdims=True))
        logits = jnp.concatenate(lines, axis=0) * (index_scale * LOG2E)
        ids = lax.broadcasted_iota(jnp.int32, logits.shape, 1) + start
        logit_ref[:, start : start + tile] = jnp.where(ids <= pos_ref[...], logits, masked_fill)
    logits = logit_ref[...]
    high = jnp.max(logits, axis=1, keepdims=True)
    total = jnp.sum(jnp.exp2(logits - high), axis=1, keepdims=True)
    line = jnp.where(diagonal(rows), high + jnp.log2(total), 0.0)
    line = jnp.sum(line, axis=0, keepdims=True)
    groups, heads, _ = own_ref.shape
    copies = stat_ref.shape[0]
    lines = [own_ref[group, head : head + 1, :] for group in range(groups) for head in range(heads)]
    for at, part in enumerate(lines + [line]):
        stat_ref[:, :, at * LANES : (at + 1) * LANES] = jnp.broadcast_to(
            part[None], (copies, 1, LANES)
        )


def index_logits(row_pos, q, w, k, own, copies):
    rows, iheads, width = q.shape
    keys = k.shape[0]
    return pl.pallas_call(
        index_logits_kernel,
        out_shape=(
            pltpu.HBM((rows, keys), jnp.float32),
            pltpu.HBM((copies, 1, own.size + LANES), jnp.float32),
        ),
        compiler_params=pltpu.CompilerParams(vmem_limit_bytes=16 * 1024 * 1024),
        cost_estimate=pl.CostEstimate(
            flops=2 * rows * iheads * keys * width, transcendentals=rows * keys, bytes_accessed=1 << 20
        ),
        name="index_logits",
    )(row_pos.reshape(rows, 1), q.reshape(rows * iheads, width), w, k, own)


def gradients_kernel(half_ref, parts_ref, logit_ref, stat_ref, q_ref, w_ref, k_ref, *refs, count, before, row_part, key_part):
    refs = list(refs)
    before_ref = refs.pop(0) if before else None
    rows_ref = refs.pop(0) if row_part else None
    keys_ref = refs.pop(0) if key_part else None
    total_ref, w_col_ref = refs
    step = pl.program_id(0)
    rows = logit_ref.shape[0]
    iheads = q_ref.shape[0] // rows

    @pl.when(step == 0)
    def _():
        line = combined(stat_ref[...])
        total_ref[...] = jnp.sum(jnp.where(diagonal(rows), line, 0.0), axis=1, keepdims=True)
        w_col_ref[...] = jnp.transpose(w_ref[...])

    target = jnp.sum(parts_ref[...], axis=0)
    probs = jnp.exp2(logit_ref[...] - total_ref[...])
    slope = (probs - target) * count
    k = k_ref[...]
    w = w_col_ref[...]
    dots = dot(q_ref[...], k, NT)
    coefs = []
    for row in range(rows):
        own = dots[row * iheads : (row + 1) * iheads, :]
        coef = jnp.where(own > 0, slope[row : row + 1, :] * w[:, row : row + 1] * index_scale, 0.0)
        coefs.append(coef.astype(jnp.bfloat16))
    coef = jnp.concatenate(coefs, axis=0)
    if key_part:
        grad_keys = dot(coef, q_ref[...], TN)
        near, far, share, _ = keys_ref.shape
        for other in range(far):
            for side in range(near):
                at = (other * near + side) * share
                keys_ref[side, other] = grad_keys[at : at + share, :]
    if row_part:
        part = dot(coef, k, NN)

        @pl.when(step == 0)
        def _():
            rows_ref[...] = before_ref[...] + part if before else part

        @pl.when(step > 0)
        def _():
            rows_ref[...] += part


def gradients(mine, other_keys, parts, logits, stats, q, w, k, before, count, sizes, row_part, key_part):
    rows, iheads, width = q.shape
    keys = parts.shape[2]
    flat = rows * iheads
    _, nf, nz = sizes
    share = keys // (nf * nz)
    far = nf // 2
    tile = far * nz * share
    last = stats.shape[2] // LANES - 1

    def part(mine):
        return 1 - mine[0] if other_keys else mine[0]

    operands = [parts, logits, stats, q.reshape(flat, width), w, k]
    in_specs = [
        pl.BlockSpec((parts.shape[0], rows, tile), lambda t, half: (0, 0, t)),
        pl.BlockSpec((rows, tile), lambda t, mine: (0, part(mine) * 2 + t)),
        pl.BlockSpec((stats.shape[0], 1, LANES), lambda t, half: (0, 0, last)),
        pl.BlockSpec((flat, width), lambda t, half: (0, 0)),
        pl.BlockSpec((rows, iheads), lambda t, half: (0, 0)),
        pl.BlockSpec((tile, width), lambda t, mine: (part(mine) * 2 + t, 0)),
    ]
    row_spec = pl.BlockSpec((flat, width), lambda t, half: (0, 0))
    if before is not None:
        operands.append(before)
        in_specs.append(row_spec)
    out_specs, out_shape = [], []
    if row_part:
        out_specs.append(row_spec)
        out_shape.append(jax.ShapeDtypeStruct((flat, width), jnp.float32))
    if key_part:
        out_specs.append(pl.BlockSpec((nz, far, share, width), lambda t, half: (0, t, 0, 0)))
        out_shape.append(jax.ShapeDtypeStruct((nz, nf, share, width), jnp.float32))
    return pl.pallas_call(
        functools.partial(
            gradients_kernel, count=float(count), before=before is not None, row_part=row_part, key_part=key_part
        ),
        grid_spec=pltpu.PrefetchScalarGridSpec(
            num_scalar_prefetch=1,
            grid=(keys // tile,),
            in_specs=in_specs,
            out_specs=out_specs,
            scratch_shapes=[pltpu.VMEM((rows, 1), jnp.float32), pltpu.VMEM((iheads, rows), jnp.float32)],
        ),
        out_shape=out_shape,
        compiler_params=params(),
        cost_estimate=pl.CostEstimate(
            flops=(2 + 2 * row_part + 2 * key_part) * flat * keys * width,
            transcendentals=rows * keys,
            bytes_accessed=2 << 20,
        ),
        name="gradients",
    )(mine, parts, in_hbm(logits), *operands[2:])


def sum_copies_kernel(parts_ref, out_ref):
    total = jnp.sum(parts_ref[...], axis=0)
    out_ref[...] = jnp.broadcast_to(total[None], out_ref.shape)


def sum_copies(parts, copies):
    return pl.pallas_call(
        sum_copies_kernel,
        out_shape=jax.ShapeDtypeStruct((copies, *parts.shape[1:]), parts.dtype),
        compiler_params=pltpu.CompilerParams(vmem_limit_bytes=8 * 1024 * 1024),
        name="sum_copies",
    )(parts)


def exchanged(parts, axis):
    return lax.all_to_all(parts, axis, split_axis=0, concat_axis=0, tiled=True)


def at_owner(parts, axis):
    size = lax.axis_size(axis)
    own = lax.axis_index(axis)
    total = lax.dynamic_index_in_dim(parts, own, 0, keepdims=False)
    got = []
    for hop in range(1, size):
        part = lax.dynamic_index_in_dim(parts, own ^ hop, 0, keepdims=False)
        got.append(lax.ppermute(part, axis, [(i, i ^ hop) for i in range(size)]))
    return sum(got, total)


def shards(query_pos, mla_query, latent_keys, index_query, index_keys, index_weights):
    keys = latent_keys.shape[0]
    rows = index_query.shape[0]
    rel_pos = query_pos - lax.axis_index(KEY) * keys
    row_pos = lax.dynamic_slice_in_dim(rel_pos, lax.axis_index(HEAD) * rows, rows, 0)
    mine = in_hbm(lax.axis_index("yl").astype(jnp.int32).reshape(1))
    q = jnp.swapaxes(mla_query, 1, 2)
    k = jnp.swapaxes(latent_keys, 0, 1)
    sizes = [lax.axis_size(axis) for axis in HEAD]
    own_stats, q_rows = score_stats(rel_pos, q, k)
    logits, own_stats = index_logits(
        row_pos, index_query, index_weights, index_keys, own_stats, lax.axis_size(KEY)
    )
    stats = exchanged(own_stats, KEY)
    swap = [(0, 1), (1, 0)]

    grad_rows, grad_keys = None, []
    shares = {}
    for name, first in (("sent", False), ("kept", True)):
        for turn in range(2):
            shares[name, turn] = head_share(
                mine, name == "sent", first == (turn == 0), stats, rel_pos, q_rows, k
            )
    for turn in range(2):
        near = lax.ppermute(shares["sent", turn], "yl", swap)
        near = (near + shares["kept", turn]).reshape(-1, rows, keys // 2)
        parts = exchanged(near, RING)

        def grads(rows_before, row_part, key_part):
            return gradients(
                mine, turn == 0, parts, logits, stats, index_query, index_weights, index_keys, rows_before,
                lax.axis_size(KEY) * keys, sizes, row_part, key_part,
            )

        if turn == 0:
            grad_rows, part = grads(None, True, True)
        else:
            (grad_rows,) = grads(grad_rows, True, False)
        if turn == 1:
            (part,) = grads(None, False, True)
        grad_keys.append(part)
    near = lax.ppermute(grad_keys[0], "yl", swap)
    near = near + grad_keys[1]
    near = at_owner(near, "zl")
    key_grads = at_owner(near, "zh")
    side = lax.axis_size(SIDE)
    total = exchanged(grad_rows.reshape(side, -1, grad_rows.shape[1]), SIDE)
    total = exchanged(sum_copies(total, lax.axis_size("yh")), "yh")
    query_grads = exchanged(sum_copies(total, side).reshape(index_query.shape), SIDE)
    return (query_grads, key_grads)


def solution(mesh):
    finer = Mesh(mesh.devices.reshape(2, 4, 2, 4, 4, 2), HEAD + KEY)
    return jax.shard_map(
        shards,
        mesh=finer,
        in_specs=(
            P(),
            P(HEAD, None, None),
            P(KEY, None),
            P(HEAD, None, None),
            P(KEY, None),
            P(HEAD, None),
        ),
        out_specs=(P(HEAD, None, None), P(KEY + HEAD, None)),
        check_vma=False,
    )
```

```python
import functools
import math

import jax
import jax.numpy as jnp
from jax import lax
from jax.experimental import pallas as pl
from jax.experimental.pallas import tpu as pltpu
from jax.sharding import Mesh
from jax.sharding import PartitionSpec as P

HEADS = 128
LANES = 128
TILE = 512
KEY = ("x", "yh", "core")
HEAD = ("yl", "zh", "zl")
RING = ("zh", "zl")
SIDE = ("x", "core")
LOG2E = math.log2(math.e)
attn_scale = 192.0 ** (-0.5) * LOG2E
index_scale = 128.0 ** (-0.5)
masked_fill = -1e30
NT = (((1,), (1,)), ((), ()))
NN = (((1,), (0,)), ((), ()))
TN = (((0,), (0,)), ((), ()))


def in_hbm(x):
    return pltpu.with_memory_space_constraint(x, pltpu.HBM)


def in_vmem(x):
    return pltpu.with_memory_space_constraint(x, pltpu.VMEM)


def dot(a, b, dims):
    return lax.dot_general(a, b, dims, preferred_element_type=jnp.float32)


def params(mebibytes=24):
    return pltpu.CompilerParams(
        dimension_semantics=("arbitrary",), vmem_limit_bytes=mebibytes * 1024 * 1024
    )


def score_stats_kernel(pos_ref, q_ref, k_ref, out_ref, rows_ref, high_ref, sum_ref):
    step = pl.program_id(0)
    heads, rows, _ = rows_ref.shape
    tile = k_ref.shape[1]
    ids = lax.broadcasted_iota(jnp.int32, (rows, LANES), 1)
    past = ids + step * tile - jnp.broadcast_to(pos_ref[...], (rows, LANES))
    k = k_ref[...]

    def over_heads(first):
        for head in range(heads):
            if first:
                q = jnp.transpose(q_ref[head])
                rows_ref[head] = q
            else:
                q = rows_ref[head]
            scores = dot(q, k, NN)
            lines = [
                jnp.where(past <= -at, scores[:, at : at + LANES] * attn_scale, masked_fill)
                for at in range(0, tile, LANES)
            ]
            if first:
                high = functools.reduce(jnp.maximum, lines)
                total = sum(jnp.exp2(line - high) for line in lines)
            else:
                before = high_ref[head]
                high = functools.reduce(jnp.maximum, lines, before)
                total = sum_ref[head] * jnp.exp2(before - high) + sum(
                    jnp.exp2(line - high) for line in lines
                )
            high_ref[head] = high
            sum_ref[head] = total

    @pl.when(step == 0)
    def _():
        over_heads(True)

    @pl.when(step > 0)
    def _():
        over_heads(False)

    @pl.when(step == pl.num_programs(0) - 1)
    def _():
        cols = jnp.zeros((rows, LANES), jnp.float32)
        for head in range(heads):
            high = high_ref[head]
            most = jnp.max(high, axis=1, keepdims=True)
            total = jnp.sum(sum_ref[head] * jnp.exp2(high - most), axis=1, keepdims=True)
            cols = jnp.where(ids == head, most + jnp.log2(total), cols)
        for at in range(0, rows, LANES):
            out_ref[at // LANES] = jnp.transpose(cols[at : at + LANES, :])[:heads, :]


def score_stats(rel_pos, q, k):
    heads, width, rows = q.shape
    keys = k.shape[1]
    return pl.pallas_call(
        score_stats_kernel,
        grid=(keys // TILE,),
        in_specs=[
            pl.BlockSpec((rows, 1), lambda t: (0, 0)),
            pl.BlockSpec((heads, width, rows), lambda t: (0, 0, 0), pipeline_mode=pl.Buffered(1)),
            pl.BlockSpec((width, TILE), lambda t: (0, t)),
        ],
        out_specs=(
            pl.BlockSpec((rows // LANES, heads, LANES), lambda t: (0, 0, 0)),
            pl.BlockSpec(memory_space=pltpu.VMEM),
        ),
        out_shape=(
            jax.ShapeDtypeStruct((rows // LANES, heads, LANES), jnp.float32),
            pltpu.VMEM((heads, rows, width), q.dtype),
        ),
        scratch_shapes=[pltpu.VMEM((heads, rows, LANES), jnp.float32)] * 2,
        compiler_params=params(),
        cost_estimate=pl.CostEstimate(
            flops=2 * heads * rows * keys * width, transcendentals=heads * rows * keys, bytes_accessed=6 << 20
        ),
        name="score_stats",
    )(rel_pos.reshape(rows, 1), in_hbm(q), in_hbm(k))


def combined(stats):
    high = jnp.max(stats, axis=0)
    return high + jnp.log2(jnp.sum(jnp.exp2(stats - high[None]), axis=0))


def head_share_kernel(mine_ref, stats_ref, pos_ref, q_ref, k_ref, out_ref, col_ref, *, other_rows, other_keys):
    step = pl.program_id(0)
    heads = q_ref.shape[0]
    rows, tile = out_ref.shape
    mine = mine_ref[0]

    @pl.when(step == 0)
    def _():
        line = combined(stats_ref[...]) + math.log2(HEADS)
        lines = [line[:, head * rows : (head + 1) * rows] for head in range(heads)]
        col_ref[:, :heads] = jnp.transpose(jnp.concatenate(lines, axis=0))

    own = pl.ds(pl.multiple_of((1 - mine if other_rows else mine) * rows, rows), rows)
    k = k_ref[...]
    total = None
    for head in range(heads):
        scores = dot(q_ref[head, own, :], k, NN)
        part = jnp.exp2(scores * attn_scale - col_ref[:, head : head + 1])
        total = part if total is None else total + part
    half = 1 - mine if other_keys else mine
    ids = lax.broadcasted_iota(jnp.int32, total.shape, 1) + (half * pl.num_programs(0) + step) * tile
    out_ref[...] = jnp.where(ids <= pos_ref[...], total, 0.0)


def head_share(mine, other_rows, other_keys, stats, rel_pos, q, k):
    heads, rows, width = q.shape
    rows //= 2
    keys = k.shape[1] // 2
    steps = keys // TILE

    def rows_half(mine):
        return 1 - mine[0] if other_rows else mine[0]

    def keys_half(mine):
        return 1 - mine[0] if other_keys else mine[0]

    return pl.pallas_call(
        functools.partial(head_share_kernel, other_rows=other_rows, other_keys=other_keys),
        grid_spec=pltpu.PrefetchScalarGridSpec(
            num_scalar_prefetch=1,
            grid=(steps,),
            in_specs=[
                pl.BlockSpec((stats.shape[0], 1, heads * rows), lambda t, mine: (0, 0, rows_half(mine))),
                pl.BlockSpec((rows, 1), lambda t, mine: (rows_half(mine), 0)),
                pl.BlockSpec(memory_space=pltpu.VMEM),
                pl.BlockSpec((width, TILE), lambda t, mine: (0, keys_half(mine) * steps + t)),
            ],
            out_specs=pl.BlockSpec((rows, TILE), lambda t, mine: (0, t)),
            scratch_shapes=[pltpu.VMEM((rows, LANES), jnp.float32)],
        ),
        out_shape=jax.ShapeDtypeStruct((rows, keys), jnp.float32),
        compiler_params=params(12),
        cost_estimate=pl.CostEstimate(
            flops=2 * heads * rows * keys * width, transcendentals=heads * rows * keys, bytes_accessed=3 << 20
        ),
        name="head_share",
    )(mine, stats, rel_pos.reshape(2 * rows, 1), in_vmem(q), in_hbm(k))


def diagonal(rows):
    shape = (rows, LANES)
    return lax.broadcasted_iota(jnp.int32, shape, 0) == lax.broadcasted_iota(jnp.int32, shape, 1)


def index_logits_kernel(pos_ref, q_ref, w_ref, k_ref, own_ref, logit_ref, stat_ref):
    rows = pos_ref.shape[0]
    iheads = q_ref.shape[0] // rows
    keys = k_ref.shape[0]
    tile = 512
    w = jnp.transpose(w_ref[...])
    for start in range(0, keys, tile):
        k = k_ref[start : start + tile, :]
        lines = []
        dots = jnp.maximum(dot(q_ref[...], k, NT), 0.0)
        for row in range(rows):
            own = dots[row * iheads : (row + 1) * iheads, :]
            lines.append(jnp.sum(own * w[:, row : row + 1], axis=0, keepdims=True))
        logits = jnp.concatenate(lines, axis=0) * (index_scale * LOG2E)
        ids = lax.broadcasted_iota(jnp.int32, logits.shape, 1) + start
        logit_ref[:, start : start + tile] = jnp.where(ids <= pos_ref[...], logits, masked_fill)
    logits = logit_ref[...]
    high = jnp.max(logits, axis=1, keepdims=True)
    total = jnp.sum(jnp.exp2(logits - high), axis=1, keepdims=True)
    line = jnp.where(diagonal(rows), high + jnp.log2(total), 0.0)
    line = jnp.sum(line, axis=0, keepdims=True)
    groups, heads, _ = own_ref.shape
    copies = stat_ref.shape[0]
    lines = [own_ref[group, head : head + 1, :] for group in range(groups) for head in range(heads)]
    for at, part in enumerate(lines + [line]):
        stat_ref[:, :, at * LANES : (at + 1) * LANES] = jnp.broadcast_to(
            part[None], (copies, 1, LANES)
        )


def index_logits(row_pos, q, w, k, own, copies):
    rows, iheads, width = q.shape
    keys = k.shape[0]
    return pl.pallas_call(
        index_logits_kernel,
        out_shape=(
            pltpu.HBM((rows, keys), jnp.float32),
            pltpu.HBM((copies, 1, own.size + LANES), jnp.float32),
        ),
        compiler_params=pltpu.CompilerParams(vmem_limit_bytes=16 * 1024 * 1024),
        cost_estimate=pl.CostEstimate(
            flops=2 * rows * iheads * keys * width, transcendentals=rows * keys, bytes_accessed=1 << 20
        ),
        name="index_logits",
    )(row_pos.reshape(rows, 1), q.reshape(rows * iheads, width), w, k, own)


def gradients_kernel(half_ref, parts_ref, logit_ref, stat_ref, q_ref, w_ref, k_ref, *refs, count, before, row_part, key_part):
    refs = list(refs)
    before_ref = refs.pop(0) if before else None
    rows_ref = refs.pop(0) if row_part else None
    keys_ref = refs.pop(0) if key_part else None
    total_ref, w_col_ref = refs
    step = pl.program_id(0)
    rows = logit_ref.shape[0]
    iheads = q_ref.shape[0] // rows

    @pl.when(step == 0)
    def _():
        line = combined(stat_ref[...])
        total_ref[...] = jnp.sum(jnp.where(diagonal(rows), line, 0.0), axis=1, keepdims=True)
        w_col_ref[...] = jnp.transpose(w_ref[...]) * index_scale

    target = jnp.sum(parts_ref[...], axis=0)
    probs = jnp.exp2(logit_ref[...] - total_ref[...])
    slope = (probs - target) * count
    k = k_ref[...]
    w = w_col_ref[...]
    dots = dot(q_ref[...], k, NT)
    coefs = []
    for row in range(rows):
        own = dots[row * iheads : (row + 1) * iheads, :]
        coef = jnp.where(own > 0, slope[row : row + 1, :] * w[:, row : row + 1], 0.0)
        coefs.append(coef.astype(jnp.bfloat16))
    coef = jnp.concatenate(coefs, axis=0)
    if key_part:
        grad_keys = dot(coef, q_ref[...], TN)
        near, far, share, _ = keys_ref.shape
        for other in range(far):
            for side in range(near):
                at = (other * near + side) * share
                keys_ref[side, other] = grad_keys[at : at + share, :]
    if row_part:
        part = dot(coef, k, NN)

        @pl.when(step == 0)
        def _():
            rows_ref[...] = before_ref[...] + part if before else part

        @pl.when(step > 0)
        def _():
            rows_ref[...] += part


def gradients(mine, other_keys, parts, logits, stats, q, w, k, before, count, sizes, row_part, key_part):
    rows, iheads, width = q.shape
    keys = parts.shape[2]
    flat = rows * iheads
    _, nf, nz = sizes
    share = keys // (nf * nz)
    far = nf // 2
    tile = far * nz * share if key_part else keys
    steps = keys // tile
    last = stats.shape[2] // LANES - 1

    def part(mine):
        return 1 - mine[0] if other_keys else mine[0]

    operands = [parts, logits, stats, q.reshape(flat, width), w, k]
    in_specs = [
        pl.BlockSpec((parts.shape[0], rows, tile), lambda t, half: (0, 0, t)),
        pl.BlockSpec((rows, tile), lambda t, mine: (0, part(mine) * steps + t)),
        pl.BlockSpec((stats.shape[0], 1, LANES), lambda t, half: (0, 0, last)),
        pl.BlockSpec((flat, width), lambda t, half: (0, 0)),
        pl.BlockSpec((rows, iheads), lambda t, half: (0, 0)),
        pl.BlockSpec((tile, width), lambda t, mine: (part(mine) * steps + t, 0)),
    ]
    row_spec = pl.BlockSpec((flat, width), lambda t, half: (0, 0))
    if before is not None:
        operands.append(before)
        in_specs.append(row_spec)
    out_specs, out_shape = [], []
    if row_part:
        out_specs.append(row_spec)
        out_shape.append(jax.ShapeDtypeStruct((flat, width), jnp.float32))
    if key_part:
        out_specs.append(pl.BlockSpec((nz, far, share, width), lambda t, half: (0, t, 0, 0)))
        out_shape.append(jax.ShapeDtypeStruct((nz, nf, share, width), jnp.float32))
    return pl.pallas_call(
        functools.partial(
            gradients_kernel, count=float(count), before=before is not None, row_part=row_part, key_part=key_part
        ),
        grid_spec=pltpu.PrefetchScalarGridSpec(
            num_scalar_prefetch=1,
            grid=(steps,),
            in_specs=in_specs,
            out_specs=out_specs,
            scratch_shapes=[pltpu.VMEM((rows, 1), jnp.float32), pltpu.VMEM((iheads, rows), jnp.float32)],
        ),
        out_shape=out_shape,
        compiler_params=params(),
        cost_estimate=pl.CostEstimate(
            flops=(2 + 2 * row_part + 2 * key_part) * flat * keys * width,
            transcendentals=rows * keys,
            bytes_accessed=2 << 20,
        ),
        name="gradients",
    )(mine, parts, in_hbm(logits), *operands[2:])


def sum_copies_kernel(parts_ref, out_ref):
    total = jnp.sum(parts_ref[...], axis=0)
    out_ref[...] = jnp.broadcast_to(total[None], out_ref.shape)


def sum_copies(parts, copies):
    return pl.pallas_call(
        sum_copies_kernel,
        out_shape=jax.ShapeDtypeStruct((copies, *parts.shape[1:]), parts.dtype),
        compiler_params=pltpu.CompilerParams(vmem_limit_bytes=8 * 1024 * 1024),
        name="sum_copies",
    )(parts)


def exchanged(parts, axis):
    return lax.all_to_all(parts, axis, split_axis=0, concat_axis=0, tiled=True)


def at_owner(parts, axis):
    size = lax.axis_size(axis)
    own = lax.axis_index(axis)
    total = lax.dynamic_index_in_dim(parts, own, 0, keepdims=False)
    got = []
    for hop in range(1, size):
        part = lax.dynamic_index_in_dim(parts, own ^ hop, 0, keepdims=False)
        got.append(lax.ppermute(part, axis, [(i, i ^ hop) for i in range(size)]))
    return sum(got, total)


def shards(query_pos, mla_query, latent_keys, index_query, index_keys, index_weights):
    keys = latent_keys.shape[0]
    rows = index_query.shape[0]
    rel_pos = query_pos - lax.axis_index(KEY) * keys
    row_pos = lax.dynamic_slice_in_dim(rel_pos, lax.axis_index(HEAD) * rows, rows, 0)
    mine = in_hbm(lax.axis_index("yl").astype(jnp.int32).reshape(1))
    q = jnp.swapaxes(mla_query, 1, 2)
    k = jnp.swapaxes(latent_keys, 0, 1)
    sizes = [lax.axis_size(axis) for axis in HEAD]
    own_stats, q_rows = score_stats(rel_pos, q, k)
    logits, own_stats = index_logits(
        row_pos, index_query, index_weights, index_keys, own_stats, lax.axis_size(KEY)
    )
    stats = exchanged(own_stats, KEY)
    swap = [(0, 1), (1, 0)]

    grad_rows, grad_keys = None, []
    shares = {}
    for name, first in (("sent", False), ("kept", True)):
        for turn in range(2):
            shares[name, turn] = head_share(
                mine, name == "sent", first == (turn == 0), stats, rel_pos, q_rows, k
            )
    for turn in range(2):
        near = lax.ppermute(shares["sent", turn], "yl", swap)
        near = (near + shares["kept", turn]).reshape(-1, rows, keys // 2)
        parts = exchanged(near, RING)

        def grads(rows_before, row_part, key_part):
            return gradients(
                mine, turn == 0, parts, logits, stats, index_query, index_weights, index_keys, rows_before,
                lax.axis_size(KEY) * keys, sizes, row_part, key_part,
            )

        if turn == 0:
            grad_rows, part = grads(None, True, True)
        else:
            (grad_rows,) = grads(grad_rows, True, False)
        if turn == 1:
            (part,) = grads(None, False, True)
        grad_keys.append(part)
    near = lax.ppermute(grad_keys[0], "yl", swap)
    near = near + grad_keys[1]
    near = at_owner(near, "zl")
    key_grads = at_owner(near, "zh")
    side = lax.axis_size(SIDE)
    total = exchanged(grad_rows.reshape(side, -1, grad_rows.shape[1]), SIDE)
    total = exchanged(sum_copies(total, lax.axis_size("yh")), "yh")
    query_grads = exchanged(sum_copies(total, side).reshape(index_query.shape), SIDE)
    return (query_grads, key_grads)


def solution(mesh):
    finer = Mesh(mesh.devices.reshape(2, 4, 2, 4, 4, 2), HEAD + KEY)
    return jax.shard_map(
        shards,
        mesh=finer,
        in_specs=(
            P(),
            P(HEAD, None, None),
            P(KEY, None),
            P(HEAD, None, None),
            P(KEY, None),
            P(HEAD, None),
        ),
        out_specs=(P(HEAD, None, None), P(KEY + HEAD, None)),
        check_vma=False,
    )
```

```python
import functools
import math

import jax
import jax.numpy as jnp
from jax import lax
from jax.experimental import pallas as pl
from jax.experimental.pallas import tpu as pltpu
from jax.sharding import Mesh
from jax.sharding import PartitionSpec as P

HEADS = 128
LANES = 128
TILE = 512
KEY = ("x", "yh", "core")
HEAD = ("yl", "zh", "zl")
RING = ("zh", "zl")
SIDE = ("x", "core")
LOG2E = math.log2(math.e)
attn_scale = 192.0 ** (-0.5) * LOG2E
index_scale = 128.0 ** (-0.5)
masked_fill = -1e30
NT = (((1,), (1,)), ((), ()))
NN = (((1,), (0,)), ((), ()))
TN = (((0,), (0,)), ((), ()))


def in_hbm(x):
    return pltpu.with_memory_space_constraint(x, pltpu.HBM)


def in_vmem(x):
    return pltpu.with_memory_space_constraint(x, pltpu.VMEM)


def dot(a, b, dims):
    return lax.dot_general(a, b, dims, preferred_element_type=jnp.float32)


def params(mebibytes=24):
    return pltpu.CompilerParams(
        dimension_semantics=("arbitrary",), vmem_limit_bytes=mebibytes * 1024 * 1024
    )


def score_stats_kernel(pos_ref, q_ref, k_ref, out_ref, rows_ref, high_ref, sum_ref):
    step = pl.program_id(0)
    heads, rows, _ = rows_ref.shape
    tile = k_ref.shape[1]
    ids = lax.broadcasted_iota(jnp.int32, (rows, LANES), 1)
    past = ids + step * tile - jnp.broadcast_to(pos_ref[...], (rows, LANES))
    k = k_ref[...]

    def over_heads(first):
        for head in range(heads):
            if first:
                q = jnp.transpose(q_ref[head])
                rows_ref[head] = q
            else:
                q = rows_ref[head]
            scores = dot(q, k, NN)
            lines = [
                jnp.where(past <= -at, scores[:, at : at + LANES] * attn_scale, masked_fill)
                for at in range(0, tile, LANES)
            ]
            if first:
                high = functools.reduce(jnp.maximum, lines)
                total = sum(jnp.exp2(line - high) for line in lines)
            else:
                before = high_ref[head]
                high = functools.reduce(jnp.maximum, lines, before)
                total = sum_ref[head] * jnp.exp2(before - high) + sum(
                    jnp.exp2(line - high) for line in lines
                )
            high_ref[head] = high
            sum_ref[head] = total

    @pl.when(step == 0)
    def _():
        over_heads(True)

    @pl.when(step > 0)
    def _():
        over_heads(False)

    @pl.when(step == pl.num_programs(0) - 1)
    def _():
        cols = jnp.zeros((rows, LANES), jnp.float32)
        for head in range(heads):
            high = high_ref[head]
            most = jnp.max(high, axis=1, keepdims=True)
            total = jnp.sum(sum_ref[head] * jnp.exp2(high - most), axis=1, keepdims=True)
            cols = jnp.where(ids == head, most + jnp.log2(total), cols)
        for at in range(0, rows, LANES):
            out_ref[at // LANES] = jnp.transpose(cols[at : at + LANES, :])[:heads, :]


def score_stats(rel_pos, q, k):
    heads, width, rows = q.shape
    keys = k.shape[1]
    return pl.pallas_call(
        score_stats_kernel,
        grid=(keys // TILE,),
        in_specs=[
            pl.BlockSpec((rows, 1), lambda t: (0, 0)),
            pl.BlockSpec((heads, width, rows), lambda t: (0, 0, 0), pipeline_mode=pl.Buffered(1)),
            pl.BlockSpec((width, TILE), lambda t: (0, t)),
        ],
        out_specs=(
            pl.BlockSpec((rows // LANES, heads, LANES), lambda t: (0, 0, 0)),
            pl.BlockSpec(memory_space=pltpu.VMEM),
        ),
        out_shape=(
            jax.ShapeDtypeStruct((rows // LANES, heads, LANES), jnp.float32),
            pltpu.VMEM((heads, rows, width), q.dtype),
        ),
        scratch_shapes=[pltpu.VMEM((heads, rows, LANES), jnp.float32)] * 2,
        compiler_params=params(),
        cost_estimate=pl.CostEstimate(
            flops=2 * heads * rows * keys * width, transcendentals=heads * rows * keys, bytes_accessed=6 << 20
        ),
        name="score_stats",
    )(rel_pos.reshape(rows, 1), in_hbm(q), in_hbm(k))


def combined(stats):
    high = jnp.max(stats, axis=0)
    return high + jnp.log2(jnp.sum(jnp.exp2(stats - high[None]), axis=0))


def head_share_kernel(mine_ref, stats_ref, pos_ref, q_ref, k_ref, out_ref, col_ref, *, other_rows, other_keys):
    step = pl.program_id(0)
    heads = q_ref.shape[0]
    rows, tile = out_ref.shape
    mine = mine_ref[0]

    @pl.when(step == 0)
    def _():
        line = combined(stats_ref[...]) + math.log2(HEADS)
        lines = [line[:, head * rows : (head + 1) * rows] for head in range(heads)]
        col_ref[:, :heads] = jnp.transpose(jnp.concatenate(lines, axis=0))

    own = pl.ds(pl.multiple_of((1 - mine if other_rows else mine) * rows, rows), rows)
    k = k_ref[...]
    total = None
    for head in range(heads):
        scores = dot(q_ref[head, own, :], k, NN)
        part = jnp.exp2(scores * attn_scale - col_ref[:, head : head + 1])
        total = part if total is None else total + part
    half = 1 - mine if other_keys else mine
    ids = lax.broadcasted_iota(jnp.int32, total.shape, 1) + (half * pl.num_programs(0) + step) * tile
    out_ref[...] = jnp.where(ids <= pos_ref[...], total, 0.0)


def head_share(mine, other_rows, other_keys, stats, rel_pos, q, k):
    heads, rows, width = q.shape
    rows //= 2
    keys = k.shape[1] // 2
    steps = keys // TILE

    def rows_half(mine):
        return 1 - mine[0] if other_rows else mine[0]

    def keys_half(mine):
        return 1 - mine[0] if other_keys else mine[0]

    return pl.pallas_call(
        functools.partial(head_share_kernel, other_rows=other_rows, other_keys=other_keys),
        grid_spec=pltpu.PrefetchScalarGridSpec(
            num_scalar_prefetch=1,
            grid=(steps,),
            in_specs=[
                pl.BlockSpec((stats.shape[0], 1, heads * rows), lambda t, mine: (0, 0, rows_half(mine))),
                pl.BlockSpec((rows, 1), lambda t, mine: (rows_half(mine), 0)),
                pl.BlockSpec(memory_space=pltpu.VMEM),
                pl.BlockSpec((width, TILE), lambda t, mine: (0, keys_half(mine) * steps + t)),
            ],
            out_specs=pl.BlockSpec((rows, TILE), lambda t, mine: (0, t)),
            scratch_shapes=[pltpu.VMEM((rows, LANES), jnp.float32)],
        ),
        out_shape=jax.ShapeDtypeStruct((rows, keys), jnp.float32),
        compiler_params=params(12),
        cost_estimate=pl.CostEstimate(
            flops=2 * heads * rows * keys * width, transcendentals=heads * rows * keys, bytes_accessed=3 << 20
        ),
        name="head_share",
    )(mine, stats, rel_pos.reshape(2 * rows, 1), in_vmem(q), in_hbm(k))


def diagonal(rows):
    shape = (rows, LANES)
    return lax.broadcasted_iota(jnp.int32, shape, 0) == lax.broadcasted_iota(jnp.int32, shape, 1)


def index_logits_kernel(pos_ref, q_ref, w_ref, k_ref, own_ref, logit_ref, stat_ref):
    rows = pos_ref.shape[0]
    iheads = q_ref.shape[0] // rows
    keys = k_ref.shape[0]
    tile = 512
    w = jnp.transpose(w_ref[...])
    for start in range(0, keys, tile):
        k = k_ref[start : start + tile, :]
        lines = []
        dots = jnp.maximum(dot(q_ref[...], k, NT), 0.0)
        for row in range(rows):
            own = dots[row * iheads : (row + 1) * iheads, :]
            lines.append(jnp.sum(own * w[:, row : row + 1], axis=0, keepdims=True))
        logits = jnp.concatenate(lines, axis=0) * (index_scale * LOG2E)
        ids = lax.broadcasted_iota(jnp.int32, logits.shape, 1) + start
        logit_ref[:, start : start + tile] = jnp.where(ids <= pos_ref[...], logits, masked_fill)
    logits = logit_ref[...]
    high = jnp.max(logits, axis=1, keepdims=True)
    total = jnp.sum(jnp.exp2(logits - high), axis=1, keepdims=True)
    line = jnp.where(diagonal(rows), high + jnp.log2(total), 0.0)
    line = jnp.sum(line, axis=0, keepdims=True)
    groups, heads, _ = own_ref.shape
    copies = stat_ref.shape[0]
    lines = [own_ref[group, head : head + 1, :] for group in range(groups) for head in range(heads)]
    for at, part in enumerate(lines + [line]):
        stat_ref[:, :, at * LANES : (at + 1) * LANES] = jnp.broadcast_to(
            part[None], (copies, 1, LANES)
        )


def index_logits(row_pos, q, w, k, own, copies):
    rows, iheads, width = q.shape
    keys = k.shape[0]
    return pl.pallas_call(
        index_logits_kernel,
        out_shape=(
            pltpu.HBM((rows, keys), jnp.float32),
            pltpu.HBM((copies, 1, own.size + LANES), jnp.float32),
        ),
        compiler_params=pltpu.CompilerParams(vmem_limit_bytes=16 * 1024 * 1024),
        cost_estimate=pl.CostEstimate(
            flops=2 * rows * iheads * keys * width, transcendentals=rows * keys, bytes_accessed=1 << 20
        ),
        name="index_logits",
    )(row_pos.reshape(rows, 1), q.reshape(rows * iheads, width), w, k, own)


def gradients_kernel(half_ref, parts_ref, logit_ref, stat_ref, q_ref, w_ref, k_ref, *refs, count, before, row_part, key_part):
    refs = list(refs)
    before_ref = refs.pop(0) if before else None
    rows_ref = refs.pop(0) if row_part else None
    keys_ref = refs.pop(0) if key_part else None
    total_ref, w_col_ref = refs
    step = pl.program_id(0)
    rows = logit_ref.shape[0]
    iheads = q_ref.shape[0] // rows

    @pl.when(step == 0)
    def _():
        line = combined(stat_ref[...])
        total_ref[...] = jnp.sum(jnp.where(diagonal(rows), line, 0.0), axis=1, keepdims=True)
        w_col_ref[...] = jnp.transpose(w_ref[...]) * index_scale

    target = jnp.sum(parts_ref[...], axis=0)
    probs = jnp.exp2(logit_ref[...] - total_ref[...])
    slope = (probs - target) * count
    k = k_ref[...]
    w = w_col_ref[...]
    dots = dot(q_ref[...], k, NT)
    coefs = []
    for row in range(rows):
        own = dots[row * iheads : (row + 1) * iheads, :]
        coef = jnp.where(own > 0, slope[row : row + 1, :] * w[:, row : row + 1], 0.0)
        coefs.append(coef.astype(jnp.bfloat16))
    coef = jnp.concatenate(coefs, axis=0)
    if key_part:
        grad_keys = dot(coef, q_ref[...], TN)
        near, far, share, _ = keys_ref.shape
        for other in range(far):
            for side in range(near):
                at = (other * near + side) * share
                keys_ref[side, other] = grad_keys[at : at + share, :]
    if row_part:
        part = dot(coef, k, NN)

        @pl.when(step == 0)
        def _():
            rows_ref[...] = before_ref[...] + part if before else part

        @pl.when(step > 0)
        def _():
            rows_ref[...] += part


def gradients(mine, other_keys, parts, logits, stats, q, w, k, before, count, sizes, row_part, key_part):
    rows, iheads, width = q.shape
    keys = parts.shape[2]
    flat = rows * iheads
    _, nf, nz = sizes
    share = keys // (nf * nz)
    far = nf // 2
    tile = far * nz * share if key_part else keys
    steps = keys // tile
    last = stats.shape[2] // LANES - 1

    def part(mine):
        return 1 - mine[0] if other_keys else mine[0]

    operands = [parts, logits, stats, q.reshape(flat, width), w, k]
    in_specs = [
        pl.BlockSpec((parts.shape[0], rows, tile), lambda t, half: (0, 0, t)),
        pl.BlockSpec((rows, tile), lambda t, mine: (0, part(mine) * steps + t)),
        pl.BlockSpec((stats.shape[0], 1, LANES), lambda t, half: (0, 0, last)),
        pl.BlockSpec((flat, width), lambda t, half: (0, 0)),
        pl.BlockSpec((rows, iheads), lambda t, half: (0, 0)),
        pl.BlockSpec((tile, width), lambda t, mine: (part(mine) * steps + t, 0)),
    ]
    row_spec = pl.BlockSpec((flat, width), lambda t, half: (0, 0))
    if before is not None:
        operands.append(before)
        in_specs.append(row_spec)
    out_specs, out_shape = [], []
    if row_part:
        out_specs.append(row_spec)
        out_shape.append(jax.ShapeDtypeStruct((flat, width), jnp.float32))
    if key_part:
        out_specs.append(pl.BlockSpec((nz, far, share, width), lambda t, half: (0, t, 0, 0)))
        out_shape.append(jax.ShapeDtypeStruct((nz, nf, share, width), jnp.float32))
    return pl.pallas_call(
        functools.partial(
            gradients_kernel, count=float(count), before=before is not None, row_part=row_part, key_part=key_part
        ),
        grid_spec=pltpu.PrefetchScalarGridSpec(
            num_scalar_prefetch=1,
            grid=(steps,),
            in_specs=in_specs,
            out_specs=out_specs,
            scratch_shapes=[pltpu.VMEM((rows, 1), jnp.float32), pltpu.VMEM((iheads, rows), jnp.float32)],
        ),
        out_shape=out_shape,
        compiler_params=params(),
        cost_estimate=pl.CostEstimate(
            flops=(2 + 2 * row_part + 2 * key_part) * flat * keys * width,
            transcendentals=rows * keys,
            bytes_accessed=2 << 20,
        ),
        name="gradients",
    )(mine, parts, in_hbm(logits), *operands[2:])


def sum_copies_kernel(parts_ref, out_ref):
    total = jnp.sum(parts_ref[...], axis=0)
    out_ref[...] = jnp.broadcast_to(total[None], out_ref.shape)


def sum_copies(parts, copies):
    count, rows, width = parts.shape
    block = rows // 4
    return pl.pallas_call(
        sum_copies_kernel,
        grid=(rows // block,),
        in_specs=[pl.BlockSpec((count, block, width), lambda r: (0, r, 0))],
        out_specs=pl.BlockSpec((copies, block, width), lambda r: (0, r, 0)),
        out_shape=jax.ShapeDtypeStruct((copies, rows, width), parts.dtype),
        compiler_params=params(8),
        name="sum_copies",
    )(parts)


def exchanged(parts, axis):
    return lax.all_to_all(parts, axis, split_axis=0, concat_axis=0, tiled=True)


def at_owner(parts, axis):
    size = lax.axis_size(axis)
    own = lax.axis_index(axis)
    total = lax.dynamic_index_in_dim(parts, own, 0, keepdims=False)
    got = []
    for hop in range(1, size):
        part = lax.dynamic_index_in_dim(parts, own ^ hop, 0, keepdims=False)
        got.append(lax.ppermute(part, axis, [(i, i ^ hop) for i in range(size)]))
    return sum(got, total)


def shards(query_pos, mla_query, latent_keys, index_query, index_keys, index_weights):
    keys = latent_keys.shape[0]
    rows = index_query.shape[0]
    rel_pos = query_pos - lax.axis_index(KEY) * keys
    row_pos = lax.dynamic_slice_in_dim(rel_pos, lax.axis_index(HEAD) * rows, rows, 0)
    mine = in_hbm(lax.axis_index("yl").astype(jnp.int32).reshape(1))
    q = jnp.swapaxes(mla_query, 1, 2)
    k = jnp.swapaxes(latent_keys, 0, 1)
    sizes = [lax.axis_size(axis) for axis in HEAD]
    own_stats, q_rows = score_stats(rel_pos, q, k)
    logits, own_stats = index_logits(
        row_pos, index_query, index_weights, index_keys, own_stats, lax.axis_size(KEY)
    )
    stats = exchanged(own_stats, KEY)
    swap = [(0, 1), (1, 0)]

    grad_rows, grad_keys = None, []
    shares = {}
    for name, first in (("sent", False), ("kept", True)):
        for turn in range(2):
            shares[name, turn] = head_share(
                mine, name == "sent", first == (turn == 0), stats, rel_pos, q_rows, k
            )
    for turn in range(2):
        near = lax.ppermute(shares["sent", turn], "yl", swap)
        near = (near + shares["kept", turn]).reshape(-1, rows, keys // 2)
        parts = exchanged(near, RING)

        def grads(rows_before, row_part, key_part):
            return gradients(
                mine, turn == 0, parts, logits, stats, index_query, index_weights, index_keys, rows_before,
                lax.axis_size(KEY) * keys, sizes, row_part, key_part,
            )

        if turn == 0:
            grad_rows, part = grads(None, True, True)
        else:
            (grad_rows,) = grads(grad_rows, True, False)
        if turn == 1:
            (part,) = grads(None, False, True)
        grad_keys.append(part)
    near = lax.ppermute(grad_keys[0], "yl", swap)
    near = near + grad_keys[1]
    near = at_owner(near, "zl")
    key_grads = at_owner(near, "zh")
    side = lax.axis_size(SIDE)
    total = exchanged(grad_rows.reshape(side, -1, grad_rows.shape[1]), SIDE)
    total = exchanged(sum_copies(total, lax.axis_size("yh")), "yh")
    query_grads = exchanged(sum_copies(total, side).reshape(index_query.shape), SIDE)
    return (query_grads, key_grads)


def solution(mesh):
    finer = Mesh(mesh.devices.reshape(2, 4, 2, 4, 4, 2), HEAD + KEY)
    return jax.shard_map(
        shards,
        mesh=finer,
        in_specs=(
            P(),
            P(HEAD, None, None),
            P(KEY, None),
            P(HEAD, None, None),
            P(KEY, None),
            P(HEAD, None),
        ),
        out_specs=(P(HEAD, None, None), P(KEY + HEAD, None)),
        check_vma=False,
    )
```
